32 devices in a mesh: lon: 8 (over y, x, core), lat: 4 (over z).
Axes of the slice: x: 2, y: 2, z: 4, core: 2. Of those that a mesh axis runs over, the one named last changes fastest.
Arguments:
- initial_kelvin_map: float32 [512, 256, 128], P('lon', 'lat'), may hold values from -6 to 6
- thermal_diffusivity_map: float32 [512, 256, 128], P('lon', 'lat'), may hold values from 0.1 to 1
- interior_power_source: float32 [512, 256, 128], P('lon', 'lat'), may hold values from -6 to 6
- earlier_east_west_basis: float32 [512, 32], P('lon'), may hold values from -0.25 to 0.25
- earlier_north_south_basis: float32 [256, 32], P('lat'), may hold values from -0.375 to 0.375
- earlier_depthwise_basis: float32 [128, 32], replicated, may hold values from -0.5 to 0.5
Outputs:
- final_kelvin_map: float32 [512, 256, 128], P('lon', 'lat')
- error: float32 [512, 256, 128], P('lon', 'lat')
- new_lon: float32 [512, 32], P('lon')
- new_lat: float32 [256, 32], P('lat')
- new_rad: float32 [128, 32], replicated
- core: float32 [32, 32, 32], replicated
The draws below stay inside these ranges and needn't reach their ends.
All inputs are finite; a program needn't handle non-finite values.
Results may differ from the reference program's by a relative error of at most 0.02.
Values sent between devices are 32-bit elements; how exact they have to be, the bound alone decides.
A program may use at most 64 MiB of HBM per device.

```python
import math
import jax
import jax.numpy as jnp
from jax import lax

SHELL_LAYERS = 128
R = 32
STEPS = 4
EAST_WEST_SIZE = 512
NORTH_SOUTH_SIZE = 256


def block_scale(key, dims, split, least, top_value):
    loudness, own = 1.0, jax.random.fold_in(key, 6)
    for dim, parts in split:
        steps = jnp.exp(jax.random.uniform(jax.random.fold_in(own, dim), (parts,), jnp.float32, least / len(split), top_value / len(split)))
        loudness = loudness * jnp.repeat(steps, dims[dim] // parts).reshape([-1 if axis == dim else 1 for axis in range(len(dims))])
    return loudness


def centred(key, shape, scale, limit, split=(), dtype=jnp.bfloat16):
    entries = scale * jax.random.normal(key, shape, jnp.float32)
    if split:
        entries = entries * block_scale(key, shape, split, -0.22, 0.18)
    return jnp.clip(entries, -limit, limit).astype(dtype)


def setup_inputs(seed: int = 0) -> dict:
    key_list = jax.random.split(jax.random.key(seed), 7)
    return {
        "initial_kelvin_map": centred(key_list[0], (EAST_WEST_SIZE, NORTH_SOUTH_SIZE, SHELL_LAYERS), 1.0, 6.0, ((0, 8), (1, 4)), jnp.float32),
        "thermal_diffusivity_map": jnp.clip(jnp.exp(math.log(1.0) - 2.3025851 * jax.random.uniform(key_list[1], (EAST_WEST_SIZE, NORTH_SOUTH_SIZE, SHELL_LAYERS), jnp.float32) ** block_scale(key_list[1], (EAST_WEST_SIZE, NORTH_SOUTH_SIZE, SHELL_LAYERS), ((0, 8), (1, 4)), -0.2, 0.2)), 0.1, 1.0),
        "interior_power_source": centred(key_list[2], (EAST_WEST_SIZE, NORTH_SOUTH_SIZE, SHELL_LAYERS), 1.0, 6.0, ((0, 8), (1, 4)), jnp.float32),
        "earlier_east_west_basis": centred(key_list[3], (EAST_WEST_SIZE, R), EAST_WEST_SIZE ** -0.5, 0.25, ((0, 8),), jnp.float32),
        "earlier_north_south_basis": centred(key_list[4], (NORTH_SOUTH_SIZE, R), NORTH_SOUTH_SIZE ** -0.5, 0.375, ((0, 4),), jnp.float32),
        "earlier_depthwise_basis": centred(key_list[5], (SHELL_LAYERS, R), SHELL_LAYERS ** -0.5, 0.5, (), jnp.float32),
    }


highest = lax.Precision.HIGHEST
time_step = 0.15

def harmonic(cond_a, cond_b):
    summed = cond_a + cond_b
    return 2.0 * cond_a * cond_b / jnp.where(summed > 0.0, summed, 1.0)

def advance(padded, cond_pad, interior_power_source):
    centre = padded[1:-1, 1:-1]
    kcentre = cond_pad[1:-1, 1:-1]
    change = interior_power_source
    pairs = ((padded[2:, 1:-1], cond_pad[2:, 1:-1]), (padded[:-2, 1:-1], cond_pad[:-2, 1:-1]), (padded[1:-1, 2:], cond_pad[1:-1, 2:]), (padded[1:-1, :-2], cond_pad[1:-1, :-2]))
    for near_t, near_k in pairs:
        change = change + harmonic(kcentre, near_k) * (near_t - centre)
    radial_t = jnp.pad(centre, ((0, 0), (0, 0), (1, 1)))
    radial_k = jnp.pad(kcentre, ((0, 0), (0, 0), (1, 1)))
    change = change + harmonic(kcentre, radial_k[:, :, 2:]) * (radial_t[:, :, 2:] - centre)
    change = change + harmonic(kcentre, radial_k[:, :, :-2]) * (radial_t[:, :, :-2] - centre)
    return centre + time_step * change

def extend(values):
    wrapped = jnp.pad(values, ((1, 1), (0, 0), (0, 0)), mode='wrap')
    return jnp.pad(wrapped, ((0, 0), (1, 1), (0, 0)))

def orthonormal(block, gram):
    factor_l = jnp.linalg.cholesky(gram)
    return lax.linalg.triangular_solve(factor_l, block, left_side=False, lower=True, transpose_a=True)

def refine(modes, factor):
    proj = jnp.dot(modes.T, factor, precision=highest)
    block = jnp.dot(modes, proj, precision=highest)
    gram = jnp.dot(block.T, block, precision=highest)
    return orthonormal(block, gram)

def reference(initial_kelvin_map, thermal_diffusivity_map, interior_power_source, earlier_east_west_basis, earlier_north_south_basis, earlier_depthwise_basis):
    cond_pad = extend(thermal_diffusivity_map)
    final_kelvin_map = initial_kelvin_map
    for step_index in range(STEPS):
        final_kelvin_map = advance(extend(final_kelvin_map), cond_pad, interior_power_source)
    rad_proj = jnp.dot(final_kelvin_map.reshape(EAST_WEST_SIZE * NORTH_SOUTH_SIZE, SHELL_LAYERS), earlier_depthwise_basis, precision=highest).reshape(EAST_WEST_SIZE, NORTH_SOUTH_SIZE, R)
    modes = jnp.einsum('ijb,ja->iab', rad_proj, earlier_north_south_basis, precision=highest).reshape(EAST_WEST_SIZE, R * R)
    new_lon = refine(modes, earlier_east_west_basis)
    modes = jnp.einsum('ijb,ia->jab', rad_proj, new_lon, precision=highest).reshape(NORTH_SOUTH_SIZE, R * R)
    new_lat = refine(modes, earlier_north_south_basis)
    lon_proj = jnp.dot(new_lon.T, final_kelvin_map.reshape(EAST_WEST_SIZE, NORTH_SOUTH_SIZE * SHELL_LAYERS), precision=highest).reshape(R, NORTH_SOUTH_SIZE, SHELL_LAYERS)
    modes = jnp.einsum('ajr,jb->rab', lon_proj, new_lat, precision=highest).reshape(SHELL_LAYERS, R * R)
    new_rad = refine(modes, earlier_depthwise_basis)
    core = jnp.einsum('rab,rc->abc', modes.reshape(SHELL_LAYERS, R, R), new_rad, precision=highest)
    first = jnp.einsum('abc,rc->abr', core, new_rad, precision=highest)
    second = jnp.einsum('abr,jb->ajr', first, new_lat, precision=highest)
    recon = jnp.dot(new_lon, second.reshape(R, NORTH_SOUTH_SIZE * SHELL_LAYERS), precision=highest).reshape(EAST_WEST_SIZE, NORTH_SOUTH_SIZE, SHELL_LAYERS)
    return (final_kelvin_map, final_kelvin_map - recon, new_lon, new_lat, new_rad, core)
```

```python
import functools

import jax
import jax.numpy as jnp
from jax import lax
from jax.experimental import pallas as pl
from jax.experimental.pallas import tpu as pltpu
from jax.sharding import PartitionSpec as P

STEPS = 4
time_step = 0.15
F32 = jnp.float32
BF16 = jnp.bfloat16
NN = (((1,), (0,)), ((), ()))
NT = (((1,), (1,)), ((), ()))
TN = (((0,), (0,)), ((), ()))


def split(x):
    hi = x.astype(BF16)
    return hi, (x - hi.astype(F32)).astype(BF16)


def dot3(a, b, dims=NN):
    ah, al = a
    bh, bl = b
    d = functools.partial(lax.dot_general, dimension_numbers=dims, preferred_element_type=F32)
    return d(ah, bh) + d(ah, bl) + d(al, bh)


def mm(a, b, dims=NN):
    return dot3(split(a), split(b), dims)


def mmh(a, b, dims=NN):
    return lax.dot_general(
        a, b, dims, precision=lax.Precision.HIGHEST, preferred_element_type=F32
    )


def chol_inverse(gram):
    n = gram.shape[0]
    row = lax.broadcasted_iota(jnp.int32, (n, n), 0)
    col = lax.broadcasted_iota(jnp.int32, (n, n), 1)
    eye = jnp.where(row == col, 1.0, 0.0).astype(F32)
    m = jnp.concatenate([gram, eye], axis=1)
    rows = lax.broadcasted_iota(jnp.int32, (n, 1), 0)
    for k in range(n - 1):
        top = m[k : k + 1, :]
        factor = jnp.where(rows > k, m[:, k : k + 1] / m[k : k + 1, k : k + 1], 0.0)
        m = m - factor * top
    diag = jnp.sum(jnp.where(row == col, m[:, :n], 0.0), axis=1, keepdims=True)
    return m[:, n:] / jnp.sqrt(diag)


def block_diag(x, count):
    n = x.shape[0]
    wide = jnp.concatenate([x] * count, axis=1)
    full = jnp.concatenate([wide] * count, axis=0)
    row = lax.broadcasted_iota(jnp.int32, full.shape, 0) // n
    col = lax.broadcasted_iota(jnp.int32, full.shape, 1) // n
    return jnp.where(row == col, full, 0.0)


class Comm:
    def __init__(self, nl, nz, send_sem, recv_sem, halo_send, halo_recv):
        self.halo_send, self.halo_recv = halo_send, halo_recv
        self.nl, self.nz = nl, nz
        self.lon = lax.axis_index("lon")
        self.lat = lax.axis_index("lat")
        self.send_sem, self.recv_sem = send_sem, recv_sem
        self.phase = 0
        self.sent = []

    def start(self, axis, source, target):
        count = self.nl if axis == "lon" else self.nz
        me = self.lon if axis == "lon" else self.lat
        ph = self.phase
        self.phase += 1
        waits = []
        for d in range(1, count):
            peer = lax.rem(me + d, count)
            owner = lax.rem(me + count - d, count)
            copy = pltpu.make_async_remote_copy(
                src_ref=source(peer),
                dst_ref=target(me),
                send_sem=self.send_sem.at[ph, d],
                recv_sem=self.recv_sem.at[ph, d],
                device_id={axis: peer},
                device_id_type=pl.DeviceIdType.MESH,
            )
            copy.start()
            self.sent.append(copy)
            waits.append(
                pltpu.make_async_remote_copy(
                    src_ref=target(owner),
                    dst_ref=target(owner),
                    send_sem=self.send_sem.at[ph, d],
                    recv_sem=self.recv_sem.at[ph, d],
                    device_id={axis: peer},
                    device_id_type=pl.DeviceIdType.MESH,
                )
            )
        return waits

    def scatter(self, axis, make, source, target):
        count = self.nl if axis == "lon" else self.nz
        me = self.lon if axis == "lon" else self.lat
        ph = self.phase
        self.phase += 1
        waits = []
        for d in range(1, count):
            peer = lax.rem(me + d, count)
            owner = lax.rem(me + count - d, count)
            source[peer] = make(peer)
            ends = dict(
                send_sem=self.send_sem.at[ph, d],
                recv_sem=self.recv_sem.at[ph, d],
                device_id={axis: peer},
                device_id_type=pl.DeviceIdType.MESH,
            )
            copy = pltpu.make_async_remote_copy(
                src_ref=source.at[peer], dst_ref=target.at[me], **ends
            )
            copy.start()
            self.sent.append(copy)
            waits.append(pltpu.make_async_remote_copy(
                src_ref=target.at[owner], dst_ref=target.at[owner], **ends
            ))
        target[me] = make(me)
        return waits

    def send(self, axis, shift, k, lane, source, target):
        count = self.nl if axis == "lon" else self.nz
        me = self.lon if axis == "lon" else self.lat
        return pltpu.make_async_remote_copy(
            src_ref=source,
            dst_ref=target,
            send_sem=self.halo_send.at[k, lane],
            recv_sem=self.halo_recv.at[k, lane],
            device_id={axis: lax.rem(me + shift + count, count)},
            device_id_type=pl.DeviceIdType.MESH,
        )

    def gather(self, axis, slots):
        me = self.lon if axis == "lon" else self.lat
        return self.start(axis, lambda peer: slots.at[me], lambda owner: slots.at[owner])

    def wait(self, waits):
        for w in waits:
            w.wait_recv()

    def finish(self):
        for c in self.sent:
            c.wait_send()


def total(slots):
    out = slots[0]
    for k in range(1, slots.shape[0]):
        out = out + slots[k]
    return out


def all_reduce(comm, buf, rs, zs, ag, during=None):
    rows = rs.shape[1]
    piece = lambda ref, p: ref.at[pl.ds(pl.multiple_of(p * rows, rows), rows)]
    first = comm.start("lon", lambda peer: piece(buf, peer), lambda owner: rs.at[owner])
    rs[comm.lon] = piece(buf, comm.lon)[...]
    if during is not None:
        during[0]()
    comm.wait(first)
    zs[comm.lat] = total(rs)
    second = comm.gather("lat", zs)
    if during is not None:
        during[1]()
    comm.wait(second)
    piece(ag, comm.lon)[...] = total(zs)
    third = comm.start("lon", lambda peer: piece(ag, comm.lon), lambda owner: piece(ag, owner))
    if during is not None:
        during[2]()
    comm.wait(third)


def harmonic(cond_a, cond_b):
    summed = cond_a + cond_b
    return 2.0 * cond_a * cond_b / jnp.where(summed > 0.0, summed, 1.0)


def batched(low, high, size, values, store):
    def group(first, count):
        outs = [values(first + k) for k in range(count)]
        for k, out in enumerate(outs):
            store(first + k, out)

    trips = (high - low) // size

    @pl.loop(0, trips)
    def _(trip):
        group(low + trip * size, size)

    left = high - low - trips * size
    if left:
        group(high - left, left)


def store_in(ref):
    def store(i, value):
        ref[i] = value

    return store


def conduct(comm, t0, k_ref, q_ref, ta, tb, hx, hy, hz, edge_k, hal_lon, hal_lat, pack):
    ni, nj, nr = t0.shape
    last_step = STEPS
    has_lo, has_hi = comm.lat > 0, comm.lat < comm.nz - 1

    def exchange(k, src):
        lon_copies = (
            comm.send("lon", 1, k, 0, src.at[ni - 1], hal_lon.at[k, 0]),
            comm.send("lon", -1, k, 1, src.at[0], hal_lon.at[k, 1]),
        )
        lat_copies = (
            (has_hi, has_lo, comm.send("lat", 1, k, 2, pack.at[k, 1], hal_lat.at[k, 0])),
            (has_lo, has_hi, comm.send("lat", -1, k, 3, pack.at[k, 0], hal_lat.at[k, 1])),
        )
        for c in lon_copies:
            c.start()
        for out, _, c in lat_copies:
            pl.when(out)(c.start)

        def wait():
            for c in lon_copies:
                c.wait_recv()
            for _, into, c in lat_copies:
                pl.when(into)(c.wait_recv)

        def wait_sent():
            for c in lon_copies:
                c.wait_send()
            for out, _, c in lat_copies:
                pl.when(out)(c.wait_send)

        return wait, wait_sent

    @pl.when(comm.lat == 0)
    def _():
        for k in range(STEPS + 1):
            hal_lat[k, 0] = jnp.zeros((ni, nr), F32)

    @pl.when(comm.lat == comm.nz - 1)
    def _():
        for k in range(STEPS + 1):
            hal_lat[k, 1] = jnp.zeros((ni, nr), F32)

    pack[last_step, 0] = k_ref[:, 0, :]
    pack[last_step, 1] = k_ref[:, nj - 1, :]
    pack[0, 0] = t0[:, 0, :]
    pack[0, 1] = t0[:, nj - 1, :]
    wait_k, sent_k = exchange(last_step, k_ref)
    wait_t, sent_t = exchange(0, t0)

    row = lax.broadcasted_iota(jnp.int32, (nj, nr), 0)
    col = lax.broadcasted_iota(jnp.int32, (nj, nr), 1)

    def faces(i):
        k = k_ref[i]
        return (
            jnp.where(row == 0, 0.0, harmonic(k, pltpu.roll(k, 1, 0))),
            jnp.where(col == 0, 0.0, harmonic(k, pltpu.roll(k, 1, 1))),
        )

    def store_faces(i, values):
        hy[i], hz[i] = values

    batched(0, ni, 2, faces, store_faces)
    batched(1, ni, 4, lambda i: harmonic(k_ref[i], k_ref[i - 1]), store_in(hx))
    wait_k()
    hx[0] = harmonic(k_ref[0], hal_lon[last_step, 0])
    hx[ni] = harmonic(k_ref[ni - 1], hal_lon[last_step, 1])
    edge_k[0] = harmonic(pack[last_step, 0], hal_lat[last_step, 0])
    edge_k[1] = harmonic(pack[last_step, 1], hal_lat[last_step, 1])

    def slab(i, before, here, after):
        fx = hx[i + 1] * (after - here) - hx[i] * (here - before)
        fy = hy[i] * (here - pltpu.roll(here, 1, 0))
        fz = hz[i] * (here - pltpu.roll(here, 1, 1))
        change = q_ref[i] + fx + (pltpu.roll(fy, nj - 1, 0) - fy) + (pltpu.roll(fz, nr - 1, 1) - fz)
        return here + time_step * change

    for step in range(STEPS):
        src = t0 if step == 0 else (ta, tb)[(step - 1) % 2]
        dst = (ta, tb)[step % 2]

        batched(1, ni - 1, 4, lambda i: slab(i, src[i - 1], src[i], src[i + 1]), store_in(dst))

        wait_t()
        dst[0] = slab(0, hal_lon[step, 0], src[0], src[1])
        dst[ni - 1] = slab(ni - 1, src[ni - 2], src[ni - 1], hal_lon[step, 1])
        for side, j in ((0, 0), (1, nj - 1)):
            flux = edge_k[side] * (hal_lat[step, side] - pack[step, side])
            edge = dst[:, j, :] + time_step * flux
            dst[:, j, :] = edge
            if step < STEPS - 1:
                pack[step + 1, side] = edge
        sent_t()
        if step < STEPS - 1:
            wait_t, sent_t = exchange(step + 1, dst)
    sent_k()


def stacked(x, axis):
    n = x.shape[axis]
    both = jnp.concatenate([x, x], axis=axis)
    low = both - both.astype(BF16).astype(F32)
    return jnp.where(lax.broadcasted_iota(jnp.int32, both.shape, axis) < n, both, low).astype(BF16)


def left_operand(x):
    high, low = split(jnp.concatenate([x, x], axis=1))
    col = lax.broadcasted_iota(jnp.int32, low.shape, 1)
    low = jnp.where(col < x.shape[1], low.astype(F32), 0.0).astype(BF16)
    return jnp.concatenate([high, low], axis=0)


def fold_rows(x):
    n = x.shape[0] // 2
    return x[:n] + x[n:]


def dot1(a, b, dims=NN):
    return lax.dot_general(a, b, dims, preferred_element_type=F32)


def sweep_kernel(nl, nz, t0, k_ref, q_ref, u_ref, v_ref, w_ref,
                 temp_ref, x3, lon_ref, lat_ref, rad_ref, core_ref,
                 ta, tb, hx, hy, hz, edge_k, hal_lon, hal_lat, pack,
                 z1, z1t, xs, xh, f_ref, y1, small,
                 y2s, y2r, p2z, y3s, y3r, y3z, us,
                 b1s, b2s, b3s, g1s, g2s, buf, rs, zs, ag,
                 send_sem, recv_sem, halo_send, halo_recv, out_sem):
    comm = Comm(nl, nz, send_sem, recv_sem, halo_send, halo_recv)
    ni, nj, nr = t0.shape
    t_ref = (ta, tb)[(STEPS - 1) % 2]
    r = u_ref.shape[0]
    group = 128 // r
    blocks = r // group
    per = r // nl
    wide = per * r

    barrier = pltpu.get_barrier_semaphore()
    for d in range(1, nl):
        pl.semaphore_signal(barrier, inc=1, device_id={"lon": lax.rem(comm.lon + d, nl)},
                            device_id_type=pl.DeviceIdType.MESH)
    for d in range(1, nz):
        pl.semaphore_signal(barrier, inc=1, device_id={"lat": lax.rem(comm.lat + d, nz)},
                            device_id_type=pl.DeviceIdType.MESH)

    pl.semaphore_wait(barrier, nl + nz - 2)
    conduct(comm, t0, k_ref, q_ref, ta, tb, hx, hy, hz, edge_k, hal_lon, hal_lat, pack)
    out_copy = pltpu.make_async_copy(t_ref, temp_ref, out_sem)
    out_copy.start()

    wts = split(w_ref[...])
    ut = u_ref[...]
    vt = v_ref[...]

    def store_z1(i, value):
        z1[:, i, :] = value

    batched(0, ni, 8, lambda i: dot3(wts, split(t_ref[i]), NT), store_z1)

    lane = lambda n, w: lax.broadcasted_iota(jnp.int32, (n, w), 1) // r
    v4 = split(jnp.concatenate([vt.T] * group, axis=1))
    uts = split(ut)
    for m in range(blocks):
        out = jnp.zeros((ni, 128), F32)
        for g in range(group):
            out = jnp.where(lane(ni, 128) == g, dot3(split(z1[m * group + g]), v4), out)
        y1[m] = out
        buf[pl.ds(m * r, r), :] = dot3(uts, split(out))

    def turn(low, high):
        for b in range(low, high):
            z1t[b] = stacked(z1[b].T, 1)

    turns = tuple(functools.partial(turn, r * k // 3, r * (k + 1) // 3) for k in range(3))
    all_reduce(comm, buf, rs, zs, ag, turns)

    acc = jnp.zeros((r, ni), F32)
    for m in range(blocks):
        acc = acc + mm(ag[pl.ds(m * r, r), :], y1[m], NT)
    b1s[comm.lat] = acc
    w = comm.gather("lat", b1s)
    comm.wait(w)
    b1t = total(b1s)
    g1s[comm.lon] = mmh(b1t, b1t, NT)
    g1w = comm.gather("lon", g1s)

    bh, bl = split(jnp.concatenate([b1t] * per, axis=0).T)
    b1x = jnp.concatenate([
        jnp.concatenate([bh, bh], axis=0),
        jnp.concatenate([bl, jnp.zeros_like(bl)], axis=0),
    ], axis=1)

    def y2piece(p):
        out = jnp.zeros((nj, wide), F32)
        for g in range(per):
            both = dot1(z1t[p * per + g], b1x)
            out = jnp.where(lane(nj, wide) == g, both[:, :wide] + both[:, wide:], out)
        return out

    w = comm.scatter("lon", y2piece, y2s, y2r)
    comm.wait(g1w)
    small[0] = chol_inverse(total(g1s))
    l1 = small[0]
    bd1 = split(block_diag(mmh(l1, l1, TN), per))
    lont = mmh(l1, b1t)
    lon_ref[...] = lont
    lonx = left_operand(lont)
    comm.wait(w)
    y2 = split(total(y2r))
    p2z[comm.lat] = dot3(split(vt), y2)
    w = comm.gather("lat", p2z)

    for j in range(0, nj, 2):
        pair = jnp.concatenate([stacked(t_ref[:, j, :], 0), stacked(t_ref[:, j + 1, :], 0)], axis=1)
        out = fold_rows(dot1(lonx, pair))
        xs[:, j, :] = out[:, :nr]
        xs[:, j + 1, :] = out[:, nr:]

    comm.wait(w)
    b2s[comm.lon] = dot3(split(dot3(split(total(p2z)), bd1)), y2, NT)
    w = comm.gather("lon", b2s)
    for a in range(r):
        xh[a] = stacked(xs[a], 0)
    comm.wait(w)
    b2t = total(b2s)
    g2s[comm.lat] = mmh(b2t, b2t, NT)
    g2w = comm.gather("lat", g2s)
    b2x = left_operand(b2t)

    def y3piece(p):
        outs = []
        for g in range(0, per, 2):
            pair = jnp.concatenate([xh[p * per + g], xh[p * per + g + 1]], axis=1)
            out = fold_rows(dot1(b2x, pair))
            outs += [out[:, :nr], out[:, nr:]]
        return jnp.concatenate(outs, axis=0)

    w = comm.scatter("lon", y3piece, y3s, y3r)
    comm.wait(g2w)
    small[1] = chol_inverse(total(g2s))
    l2 = small[1]
    bd2 = split(block_diag(l2, per))
    latt = mmh(l2, b2t)
    lat_ref[...] = latt
    comm.wait(w)
    y3z[comm.lat] = dot3(bd2, split(total(y3r)))
    w = comm.gather("lat", y3z)
    comm.wait(w)
    y3 = split(total(y3z))
    p3 = dot3(wts, y3, NT)
    b3s[comm.lon] = dot3(split(p3), y3)
    w = comm.gather("lon", b3s)
    comm.wait(w)
    b3t = total(b3s)
    us[comm.lon] = dot3(split(b3t), y3, NT)
    w = comm.gather("lon", us)
    small[0] = chol_inverse(mmh(b3t, b3t, NT))
    l3 = small[0]
    radt = mmh(l3, b3t)
    rad_ref[...] = radt
    radh = split(radt)
    l3h = split(l3)
    lonb = split(lont.T)
    comm.wait(w)
    for p in range(nl):
        core = dot3(l3h, split(us[p]))
        core_ref[pl.ds(p * wide, wide), :] = core.T
        f_ref[pl.ds(p * per, per)] = dot3(split(core), radh, TN).reshape(per, r, nr)
    for b in range(r):
        x3[:, b, :] = dot3(lonb, split(f_ref[:, b, :]))
    out_copy.wait()
    comm.finish()


def error_kernel(t_ref, s_ref, lon_ref, lat_ref, rad_ref, core_ref,
                 temp_out, err_out, lon_out, lat_out, rad_out, core_out, err, sem, temp_sem):
    temp_copy = pltpu.make_async_copy(t_ref, temp_out, temp_sem)
    temp_copy.start()
    latb = split(lat_ref[...].T)
    ni = t_ref.shape[0]
    at = 8

    def chunk(c):
        part = pl.ds(c * at, at)
        return pltpu.make_async_copy(err.at[part], err_out.at[part], sem.at[c])

    @pl.loop(0, ni // at)
    def _(c):
        outs = [t_ref[c * at + k] - dot3(latb, split(s_ref[c * at + k])) for k in range(at)]
        for k, out in enumerate(outs):
            err[c * at + k] = out
        chunk(c).start()

    lon_out[...] = lon_ref[...]
    lat_out[...] = lat_ref[...]
    rad_out[...] = rad_ref[...]
    core_out[...] = core_ref[...]

    @pl.loop(0, ni // at)
    def _(c):
        chunk(c).wait()

    temp_copy.wait()


def local(t, k, q, u, v, w):
    nl, nz = lax.axis_size("lon"), lax.axis_size("lat")
    ni, nj, nr = t.shape
    r = u.shape[1]
    rows = r * r * r // 128
    piece = rows // nl
    blocks = r * r // 128
    most = max(nl, nz)
    vm = pl.BlockSpec(memory_space=pltpu.VMEM)
    sds = lambda *s: jax.ShapeDtypeStruct(s, F32)
    V = lambda *s: pltpu.VMEM(s, F32)
    phases = 13
    per = r // nl
    wide = per * r
    B = lambda *s: pltpu.VMEM(s, BF16)
    small = (sds(r, ni), sds(r, nj), sds(r, nr), sds(r * r, r))
    temp, s, lon, lat, rad, core = pl.pallas_call(
        functools.partial(sweep_kernel, nl, nz),
        out_shape=(sds(ni, nj, nr), sds(ni, r, nr)) + small,
        in_specs=[vm] * 6,
        out_specs=(pl.BlockSpec(memory_space=pl.ANY),) + (vm,) * 5,
        scratch_shapes=[
            V(ni, nj, nr), V(ni, nj, nr), V(ni + 1, nj, nr), V(ni, nj, nr), V(ni, nj, nr),
            V(2, ni, nr), V(STEPS + 1, 2, nj, nr), V(STEPS + 1, 2, ni, nr), V(STEPS + 1, 2, ni, nr),
            V(r, ni, nj), B(r, nj, 2 * ni), V(r, nj, nr), B(r, 2 * nj, nr), V(r, r, nr),
            V(blocks, ni, 128), V(2, r, r),
            V(nl, nj, wide), V(nl, nj, wide), V(nz, r, wide),
            V(nl, wide, nr), V(nl, wide, nr), V(nz, wide, nr), V(nl, r, wide),
            V(nz, r, ni), V(nl, r, nj), V(nl, r, nr),
            V(nl, r, r), V(nz, r, r),
            V(rows, 128), V(nl, piece, 128), V(nz, piece, 128), V(rows, 128),
            pltpu.SemaphoreType.DMA((phases, most)),
            pltpu.SemaphoreType.DMA((phases, most)),
            pltpu.SemaphoreType.DMA((STEPS + 1, 4)),
            pltpu.SemaphoreType.DMA((STEPS + 1, 4)),
            pltpu.SemaphoreType.DMA,
        ],
        compiler_params=pltpu.CompilerParams(
            collective_id=1, has_side_effects=True, vmem_limit_bytes=48 * 1024 * 1024
        ),
    )(t, k, q, u.T, v.T, w.T)
    anywhere = pl.BlockSpec(memory_space=pl.ANY)
    temp, err, lon, lat, rad, core = pl.pallas_call(
        error_kernel,
        out_shape=(sds(ni, nj, nr), sds(ni, nj, nr)) + small,
        in_specs=[vm] * 6,
        out_specs=(anywhere, anywhere) + (vm,) * 4,
        scratch_shapes=[
            V(ni, nj, nr), pltpu.SemaphoreType.DMA((ni // 8,)), pltpu.SemaphoreType.DMA
        ],
        compiler_params=pltpu.CompilerParams(vmem_limit_bytes=12 * 1024 * 1024),
    )(temp, s, lon, lat, rad, core)
    return temp, err, lon.T, lat.T, rad.T, core.reshape(r, r, r)


def solution(mesh):
    grid = P("lon", "lat", None)
    in_specs = (grid, grid, grid, P("lon", None), P("lat", None), P())
    out_specs = (grid, grid, P("lon", None), P("lat", None), P(), P())
    return jax.shard_map(local, mesh=mesh, in_specs=in_specs, out_specs=out_specs, check_vma=False)
```

```python
import functools

import jax
import jax.numpy as jnp
from jax import lax
from jax.experimental import pallas as pl
from jax.experimental.pallas import tpu as pltpu
from jax.sharding import PartitionSpec as P

STEPS = 4
time_step = 0.15
F32 = jnp.float32
BF16 = jnp.bfloat16
UNROLL = 6
HALVES = 2
CUT = 32
NN = (((1,), (0,)), ((), ()))
NT = (((1,), (1,)), ((), ()))
TN = (((0,), (0,)), ((), ()))


def split(x):
    hi = x.astype(BF16)
    return hi, (x - hi.astype(F32)).astype(BF16)


def dot3(a, b, dims=NN):
    ah, al = a
    bh, bl = b
    d = functools.partial(lax.dot_general, dimension_numbers=dims, preferred_element_type=F32)
    return d(ah, bh) + d(ah, bl) + d(al, bh)


def mm(a, b, dims=NN):
    return dot3(split(a), split(b), dims)


def mmh(a, b, dims=NN):
    return lax.dot_general(
        a, b, dims, precision=lax.Precision.HIGHEST, preferred_element_type=F32
    )


def reciprocal(x):
    guess = pltpu.reciprocal(x, approx=True)
    return guess * (2.0 - x * guess)


def chol_inverse(gram):
    n = gram.shape[0]
    row = lax.broadcasted_iota(jnp.int32, (n, n), 0)
    col = lax.broadcasted_iota(jnp.int32, (n, n), 1)
    eye = jnp.where(row == col, 1.0, 0.0).astype(F32)
    m = jnp.concatenate([gram, eye], axis=1)
    rows = lax.broadcasted_iota(jnp.int32, m.shape, 0)
    for k in range(0, n, 2):
        first = jnp.broadcast_to(m[:, k : k + 1], m.shape)
        second = jnp.broadcast_to(m[:, k + 1 : k + 2], m.shape)
        top = m[k : k + 1, :]
        inverse = reciprocal(first[k : k + 1, :])
        ratio = first[k + 1 : k + 2, :] * inverse
        nxt = m[k + 1 : k + 2, :] - ratio * top
        if k + 2 < n:
            pivot = second[k + 1 : k + 2, :] - ratio * first[k + 1 : k + 2, :]
            update = first * inverse * top + (second - ratio * first) * reciprocal(pivot) * nxt
            m = jnp.where(rows > k + 1, m - update, jnp.where(rows == k + 1, nxt, m))
        else:
            m = jnp.where(rows == k + 1, nxt, m)
    diag = jnp.sum(jnp.where(row == col, m[:, :n], 0.0), axis=1, keepdims=True)
    return m[:, n:] / jnp.sqrt(diag)


def block_diag(x, count):
    n = x.shape[0]
    wide = jnp.concatenate([x] * count, axis=1)
    full = jnp.concatenate([wide] * count, axis=0)
    row = lax.broadcasted_iota(jnp.int32, full.shape, 0) // n
    col = lax.broadcasted_iota(jnp.int32, full.shape, 1) // n
    return jnp.where(row == col, full, 0.0)


class Comm:
    def __init__(self, nl, nz, send_sem, recv_sem, halo_send, halo_recv):
        self.halo_send, self.halo_recv = halo_send, halo_recv
        self.nl, self.nz = nl, nz
        self.lon = lax.axis_index("lon")
        self.lat = lax.axis_index("lat")
        self.send_sem, self.recv_sem = send_sem, recv_sem
        self.phase = 0
        self.sent = []

    def start(self, axis, source, target):
        count = self.nl if axis == "lon" else self.nz
        me = self.lon if axis == "lon" else self.lat
        ph = self.phase
        self.phase += 1
        waits = []
        for d in range(1, count):
            peer = lax.rem(me + d, count)
            owner = lax.rem(me + count - d, count)
            copy = pltpu.make_async_remote_copy(
                src_ref=source(peer),
                dst_ref=target(me),
                send_sem=self.send_sem.at[ph, d],
                recv_sem=self.recv_sem.at[ph, d],
                device_id={axis: peer},
                device_id_type=pl.DeviceIdType.MESH,
            )
            copy.start()
            self.sent.append(copy)
            waits.append(
                pltpu.make_async_remote_copy(
                    src_ref=target(owner),
                    dst_ref=target(owner),
                    send_sem=self.send_sem.at[ph, d],
                    recv_sem=self.recv_sem.at[ph, d],
                    device_id={axis: peer},
                    device_id_type=pl.DeviceIdType.MESH,
                )
            )
        return waits

    def scatter(self, axis, make, source, target):
        count = self.nl if axis == "lon" else self.nz
        me = self.lon if axis == "lon" else self.lat
        ph = self.phase
        self.phase += 1
        waits = []
        for d in range(1, count):
            peer = lax.rem(me + d, count)
            owner = lax.rem(me + count - d, count)
            source[peer] = make(peer)
            ends = dict(
                send_sem=self.send_sem.at[ph, d],
                recv_sem=self.recv_sem.at[ph, d],
                device_id={axis: peer},
                device_id_type=pl.DeviceIdType.MESH,
            )
            copy = pltpu.make_async_remote_copy(
                src_ref=source.at[peer], dst_ref=target.at[me], **ends
            )
            copy.start()
            self.sent.append(copy)
            waits.append(pltpu.make_async_remote_copy(
                src_ref=target.at[owner], dst_ref=target.at[owner], **ends
            ))
        target[me] = make(me)
        return waits

    def send(self, axis, shift, k, lane, source, target):
        count = self.nl if axis == "lon" else self.nz
        me = self.lon if axis == "lon" else self.lat
        return pltpu.make_async_remote_copy(
            src_ref=source,
            dst_ref=target,
            send_sem=self.halo_send.at[k, lane],
            recv_sem=self.halo_recv.at[k, lane],
            device_id={axis: lax.rem(me + shift + count, count)},
            device_id_type=pl.DeviceIdType.MESH,
        )

    def gather(self, axis, slots):
        me = self.lon if axis == "lon" else self.lat
        return self.start(axis, lambda peer: slots.at[me], lambda owner: slots.at[owner])

    def wait(self, waits):
        for w in waits:
            w.wait_recv()

    def finish(self):
        for c in self.sent:
            c.wait_send()


def total(slots):
    out = slots[0]
    for k in range(1, slots.shape[0]):
        out = out + slots[k]
    return out


def all_reduce(comm, buf, rs, zs, ag, during=None):
    rows = rs.shape[1]
    piece = lambda ref, p: ref.at[pl.ds(pl.multiple_of(p * rows, rows), rows)]
    first = comm.start("lon", lambda peer: piece(buf, peer), lambda owner: rs.at[owner])
    rs[comm.lon] = piece(buf, comm.lon)[...]
    if during is not None:
        during[0]()
    comm.wait(first)
    zs[comm.lat] = total(rs)
    second = comm.gather("lat", zs)
    if during is not None:
        during[1]()
    comm.wait(second)
    piece(ag, comm.lon)[...] = total(zs)
    third = comm.start("lon", lambda peer: piece(ag, comm.lon), lambda owner: piece(ag, owner))
    if during is not None:
        during[2]()
    comm.wait(third)


def harmonic(cond_a, cond_b):
    summed = cond_a + cond_b
    safe = jnp.where(summed > 0.0, summed, 1.0)
    guess = pltpu.reciprocal(safe, approx=True)
    guess = guess * (2.0 - safe * guess)
    return (cond_a + cond_a) * cond_b * guess


def in_groups(low, high, size, group):
    trips = (high - low) // size

    @pl.loop(0, trips)
    def _(trip):
        group(low + trip * size, size)

    left = high - low - trips * size
    if left:
        group(high - left, left)


def batched(low, high, size, values, store):
    def group(first, count):
        outs = [values(first + k) for k in range(count)]
        for k, out in enumerate(outs):
            store(first + k, out)

    in_groups(low, high, size, group)


def store_in(ref):
    def store(i, value):
        ref[i] = value

    return store


def conduct(comm, t0, k_ref, q_ref, ta, tb, hx, hy, hz, edge_k, hal_lon, hal_lat, pack, plane, wait_q):
    ni, nj, nr = t0.shape
    last = STEPS
    has_lo, has_hi = comm.lat > 0, comm.lat < comm.nz - 1
    sides = ((0, 0, 1), (1, nj - 1, nj - 2))

    def exchange_lat(k):
        copies = (
            (has_hi, has_lo, comm.send("lat", 1, k, 2, pack.at[k, 1], hal_lat.at[k, 0])),
            (has_lo, has_hi, comm.send("lat", -1, k, 3, pack.at[k, 0], hal_lat.at[k, 1])),
        )
        for out, _, c in copies:
            pl.when(out)(c.start)
        return copies

    def exchange_lon(k, src):
        copies = (
            comm.send("lon", 1, k, 0, src.at[ni - 1], hal_lon.at[k, 0]),
            comm.send("lon", -1, k, 1, src.at[0], hal_lon.at[k, 1]),
        )
        for c in copies:
            c.start()
        return copies

    def wait(lat_copies, lon_copies):
        for c in lon_copies:
            c.wait_recv()
        for _, into, c in lat_copies:
            pl.when(into)(c.wait_recv)

    def wait_sent(lat_copies, lon_copies):
        for c in lon_copies:
            c.wait_send()
        for out, _, c in lat_copies:
            pl.when(out)(c.wait_send)

    for side, j, _ in sides:
        pack[last, side] = k_ref[:, j, :]
        pack[0, side] = t0[:, j, :]
    sent_k = exchange_lat(last), exchange_lon(last, k_ref)
    sent_t = exchange_lat(0), exchange_lon(0, t0)

    @pl.when(comm.lat == 0)
    def _():
        for k in range(STEPS + 1):
            hal_lat[k, 0] = jnp.zeros((ni, nr), F32)

    @pl.when(comm.lat == comm.nz - 1)
    def _():
        for k in range(STEPS + 1):
            hal_lat[k, 1] = jnp.zeros((ni, nr), F32)

    row = lax.broadcasted_iota(jnp.int32, (nj, nr), 0)
    col = lax.broadcasted_iota(jnp.int32, (nj, nr), 1)
    plane_row = lax.broadcasted_iota(jnp.int32, (ni, nr), 0)

    def faces(i):
        k = k_ref[i]
        return (
            jnp.where(row == 0, 0.0, harmonic(k, pltpu.roll(k, 1, 0))),
            jnp.where(col == 0, 0.0, harmonic(k, pltpu.roll(k, 1, 1))),
        )

    def store_faces(i, values):
        hy[i], hz[i] = values

    batched(0, ni, 2, faces, store_faces)
    batched(1, ni, 4, lambda i: harmonic(k_ref[i], k_ref[i - 1]), store_in(hx))
    wait_q()
    wait(*sent_k)
    hx[0] = harmonic(k_ref[0], hal_lon[last, 0])
    hx[ni] = harmonic(k_ref[ni - 1], hal_lon[last, 1])
    for side, j, inner in sides:
        edge_k[side] = harmonic(pack[last, side], hal_lat[last, side])
        plane[side, 0] = q_ref[:, j, :]
        plane[side, 1] = hx[pl.ds(0, ni), j, :]
        plane[side, 2] = hx[pl.ds(1, ni), j, :]
        plane[side, 3] = hy[:, max(j, inner), :]
        plane[side, 4] = hz[:, j, :]

    def radial(h, here):
        flux = h * (here - pltpu.roll(here, 1, 1))
        return pltpu.roll(flux, nr - 1, 1) - flux

    def slab(i, here, before_flux, after_flux):
        fy = hy[i] * (here - pltpu.roll(here, 1, 0))
        change = q_ref[i] + (after_flux - before_flux)
        change = change + (pltpu.roll(fy, nj - 1, 0) - fy) + radial(hz[i], here)
        return here + time_step * change

    buffers = lambda step: (t0 if step == 0 else (ta, tb)[(step - 1) % 2], (ta, tb)[step % 2])
    slot = lambda step: step + (step >= last)

    def inside(step):
        src, dst = buffers(step)

        def group(first, count):
            cells = [src[first - 1 + n] for n in range(count + 2)]
            fluxes = [hx[first + n] * (cells[n + 1] - cells[n]) for n in range(count + 1)]
            outs = [slab(first + n, cells[n + 1], fluxes[n], fluxes[n + 1]) for n in range(count)]
            for n, out in enumerate(outs):
                dst[first + n] = out

        in_groups(1, ni - 1, UNROLL, group)

    def edges(step, more):
        src, dst = buffers(step)
        for side, j, inner in sides:
            here = pack[step, side]
            before = jnp.where(plane_row == 0, hal_lon[step, 0, pl.ds(j, 1), :], pltpu.roll(here, 1, 0))
            after = jnp.where(plane_row == ni - 1, hal_lon[step, 1, pl.ds(j, 1), :], pltpu.roll(here, ni - 1, 0))
            change = plane[side, 0] + plane[side, 2] * (after - here) - plane[side, 1] * (here - before)
            change = change + plane[side, 3] * (src[:, inner, :] - here)
            change = change + edge_k[side] * (hal_lat[step, side] - here) + radial(plane[side, 4], here)
            pack[slot(step + 1), side] = here + time_step * change
        lat_copies = exchange_lat(step + 1) if more else ()
        for i, before, after in (
            (0, hal_lon[step, 0], src[1]), (ni - 1, src[ni - 2], hal_lon[step, 1])
        ):
            here = src[i]
            dst[i] = slab(i, here, hx[i] * (here - before), hx[i + 1] * (after - here))
            for side, j, _ in sides:
                dst[i, pl.ds(j, 1), :] = pack[slot(step + 1), side, pl.ds(i, 1), :]
        lon_copies = exchange_lon(step + 1, dst) if more else ()
        return lat_copies, lon_copies

    def seam(step):
        dst = buffers(step)[1]
        for side, j, _ in sides:
            dst[pl.ds(1, ni - 2), j, :] = pack[slot(step + 1), side, pl.ds(1, ni - 2), :]

    for step in range(STEPS):
        if step > 0:
            inside(step)
        wait(*sent_t)
        going = edges(step, step < STEPS - 1)
        if step == 0:
            inside(step)
        seam(step)
        wait_sent(*sent_t)
        sent_t = going
    wait_sent(*sent_k)


def stacked(x, axis):
    n = x.shape[axis]
    both = jnp.concatenate([x, x], axis=axis)
    low = both - both.astype(BF16).astype(F32)
    return jnp.where(lax.broadcasted_iota(jnp.int32, both.shape, axis) < n, both, low).astype(BF16)


def left_operand(x):
    high, low = split(jnp.concatenate([x, x], axis=1))
    col = lax.broadcasted_iota(jnp.int32, low.shape, 1)
    low = jnp.where(col < x.shape[1], low.astype(F32), 0.0).astype(BF16)
    return jnp.concatenate([high, low], axis=0)


def fold_rows(x):
    n = x.shape[0] // 2
    return x[:n] + x[n:]


def dot1(a, b, dims=NN):
    return lax.dot_general(a, b, dims, preferred_element_type=F32)


def sweep_kernel(nl, nz, t_in, k_in, q_in, u_in, v_in, w_in,
                 temp_ref, x3, lon_ref, lat_ref, rad_ref, core_ref,
                 k_ref, q_ref, u_ref, v_ref, w_ref,
                 ta, tb, hx, hy, hz, edge_k, hal_lon, hal_lat, pack, plane,
                 z1, z1t, xs, xh, f_ref, y1, small,
                 y2s, y2r, p2z, y3s, y3r, y3z, us,
                 b1s, b2s, b3s, g1s, g2s, buf, rs, zs, ag,
                 send_sem, recv_sem, halo_send, halo_recv, out_sem, in_sem):
    comm = Comm(nl, nz, send_sem, recv_sem, halo_send, halo_recv)
    t0 = tb
    ni, nj, nr = t0.shape
    t_ref = (ta, tb)[(STEPS - 1) % 2]
    r = u_ref.shape[0]
    group = 128 // r
    blocks = r // group
    per = r // nl
    wide = per * r

    fetches = {}
    for n, (source, target) in enumerate((
        (t_in, t0), (k_in, k_ref), (q_in, q_ref), (u_in, u_ref), (v_in, v_ref), (w_in, w_ref)
    )):
        fetches[n] = [pltpu.make_async_copy(source, target, in_sem.at[n, 0])]
        if n < 3:
            part = ni // 4
            fetches[n] = [
                pltpu.make_async_copy(
                    source.at[pl.ds(part * c, part)], target.at[pl.ds(part * c, part)], in_sem.at[n, c]
                )
                for c in range(4)
            ]

    def fetched(*wanted):
        for n in wanted:
            for c in fetches[n]:
                c.wait()

    barrier = pltpu.get_barrier_semaphore()
    for d in range(1, nl):
        pl.semaphore_signal(barrier, inc=1, device_id={"lon": lax.rem(comm.lon + d, nl)},
                            device_id_type=pl.DeviceIdType.MESH)
    for d in range(1, nz):
        pl.semaphore_signal(barrier, inc=1, device_id={"lat": lax.rem(comm.lat + d, nz)},
                            device_id_type=pl.DeviceIdType.MESH)
    for n in (1, 0, 2, 3, 4, 5):
        for c in fetches[n]:
            c.start()
    fetched(1, 0)

    pl.semaphore_wait(barrier, nl + nz - 2)
    conduct(comm, t0, k_ref, q_ref, ta, tb, hx, hy, hz, edge_k, hal_lon, hal_lat, pack, plane,
            lambda: fetched(2, 3, 4, 5))
    out_copy = pltpu.make_async_copy(t_ref, temp_ref, out_sem)
    out_copy.start()

    wts = split(w_ref[...])
    ut = u_ref[...]
    vt = v_ref[...]

    def store_z1(i, value):
        z1[:, i, :] = value

    batched(0, ni, 8, lambda i: dot3(wts, split(t_ref[i]), NT), store_z1)

    lane = lambda n, w: lax.broadcasted_iota(jnp.int32, (n, w), 1) // r
    v4 = split(jnp.concatenate([vt.T] * group, axis=1))
    uts = split(ut)
    for m in range(blocks):
        out = jnp.zeros((ni, 128), F32)
        for g in range(group):
            out = jnp.where(lane(ni, 128) == g, dot3(split(z1[m * group + g]), v4), out)
        y1[m] = out
        buf[pl.ds(m * r, r), :] = dot3(uts, split(out))

    def turn(low, high):
        for b in range(low, high):
            z1t[b] = stacked(z1[b].T, 1)

    turns = tuple(functools.partial(turn, r * k // 3, r * (k + 1) // 3) for k in range(3))
    all_reduce(comm, buf, rs, zs, ag, turns)

    acc = jnp.zeros((r, ni), F32)
    for m in range(blocks):
        acc = acc + mm(ag[pl.ds(m * r, r), :], y1[m], NT)
    b1s[comm.lat] = acc
    w = comm.gather("lat", b1s)
    comm.wait(w)
    b1t = total(b1s)
    g1s[comm.lon] = mmh(b1t, b1t, NT)
    g1w = comm.gather("lon", g1s)

    bh, bl = split(jnp.concatenate([b1t] * per, axis=0).T)
    b1x = jnp.concatenate([
        jnp.concatenate([bh, bh], axis=0),
        jnp.concatenate([bl, jnp.zeros_like(bl)], axis=0),
    ], axis=1)

    def y2piece(p):
        out = jnp.zeros((nj, wide), F32)
        for g in range(per):
            both = dot1(z1t[p * per + g], b1x)
            out = jnp.where(lane(nj, wide) == g, both[:, :wide] + both[:, wide:], out)
        return out

    w = comm.scatter("lon", y2piece, y2s, y2r)
    comm.wait(w)
    y2 = split(total(y2r))
    p2z[comm.lat] = dot3(split(vt), y2)
    w = comm.gather("lat", p2z)
    comm.wait(g1w)
    small[0] = chol_inverse(total(g1s))
    l1 = small[0]
    bd1 = split(block_diag(mmh(l1, l1, TN), per))
    lont = mmh(l1, b1t)
    lon_ref[...] = lont
    lonx = left_operand(lont)

    def contract_lon(low, high):
        for j in range(low, high, 2):
            pair = jnp.concatenate(
                [stacked(t_ref[:, j, :], 0), stacked(t_ref[:, j + 1, :], 0)], axis=1
            )
            out = fold_rows(dot1(lonx, pair))
            xs[:, j, :] = out[:, :nr]
            xs[:, j + 1, :] = out[:, nr:]

    contract_lon(0, CUT)
    comm.wait(w)
    b2s[comm.lon] = dot3(split(dot3(split(total(p2z)), bd1)), y2, NT)
    w = comm.gather("lon", b2s)
    contract_lon(CUT, nj)
    for a in range(r):
        xh[a] = stacked(xs[a], 0)
    comm.wait(w)
    b2t = total(b2s)
    g2s[comm.lat] = mmh(b2t, b2t, NT)
    g2w = comm.gather("lat", g2s)
    b2x = left_operand(b2t)
    half = per // HALVES

    def y3piece(h, p):
        outs = []
        first = p * per + h * half
        for g in range(0, half, 2):
            mates = [xh[first + k] for k in range(g, min(g + 2, half))]
            out = fold_rows(dot1(b2x, jnp.concatenate(mates, axis=1)))
            outs += [out[:, nr * k : nr * (k + 1)] for k in range(len(mates))]
        return jnp.concatenate(outs, axis=0)

    ws = [
        comm.scatter("lon", functools.partial(y3piece, h), y3s.at[h], y3r.at[h])
        for h in range(HALVES)
    ]
    for h in range(HALVES):
        comm.wait(ws[h])
        y3z[h, comm.lat] = total(y3r.at[h])
        ws[h] = comm.gather("lat", y3z.at[h])
    comm.wait(g2w)
    small[1] = chol_inverse(total(g2s))
    l2 = small[1]
    bd2 = split(block_diag(l2, per))
    latt = mmh(l2, b2t)
    lat_ref[...] = latt
    for w in ws:
        comm.wait(w)
    whole = jnp.concatenate([total(y3z.at[h]) for h in range(HALVES)], axis=0)
    y3 = split(dot3(bd2, split(whole)))
    p3 = dot3(wts, y3, NT)
    b3s[comm.lon] = dot3(split(p3), y3)
    w = comm.gather("lon", b3s)
    comm.wait(w)
    b3t = total(b3s)
    us[comm.lon] = dot3(split(b3t), y3, NT)
    w = comm.gather("lon", us)
    small[0] = chol_inverse(mmh(b3t, b3t, NT))
    l3 = small[0]
    radt = mmh(l3, b3t)
    rad_ref[...] = radt
    radh = split(radt)
    l3h = split(l3)
    lonb = split(lont.T)
    comm.wait(w)
    for p in range(nl):
        core = dot3(l3h, split(us[p]))
        core_ref[pl.ds(p * wide, wide), :] = core.T
        f_ref[pl.ds(p * per, per)] = dot3(split(core), radh, TN).reshape(per, r, nr)
    for b in range(r):
        x3[:, b, :] = dot3(lonb, split(f_ref[:, b, :]))
    out_copy.wait()
    comm.finish()


def error_kernel(t_ref, s_ref, lon_ref, lat_ref, rad_ref, core_ref,
                 temp_out, err_out, lon_out, lat_out, rad_out, core_out, err, sem, temp_sem):
    temp_copy = pltpu.make_async_copy(t_ref, temp_out, temp_sem)
    temp_copy.start()
    latb = split(lat_ref[...].T)
    ni = t_ref.shape[0]
    at = 8

    def chunk(c):
        part = pl.ds(c * at, at)
        return pltpu.make_async_copy(err.at[part], err_out.at[part], sem.at[c])

    @pl.loop(0, ni // at)
    def _(c):
        outs = [t_ref[c * at + k] - dot3(latb, split(s_ref[c * at + k])) for k in range(at)]
        for k, out in enumerate(outs):
            err[c * at + k] = out
        chunk(c).start()

    lon_out[...] = lon_ref[...]
    lat_out[...] = lat_ref[...]
    rad_out[...] = rad_ref[...]
    core_out[...] = core_ref[...]

    @pl.loop(0, ni // at)
    def _(c):
        chunk(c).wait()

    temp_copy.wait()


def local(t, k, q, u, v, w):
    nl, nz = lax.axis_size("lon"), lax.axis_size("lat")
    ni, nj, nr = t.shape
    r = u.shape[1]
    rows = r * r * r // 128
    piece = rows // nl
    blocks = r * r // 128
    most = max(nl, nz)
    vm = pl.BlockSpec(memory_space=pltpu.VMEM)
    sds = lambda *s: jax.ShapeDtypeStruct(s, F32)
    V = lambda *s: pltpu.VMEM(s, F32)
    phases = 11 + 2 * HALVES
    per = r // nl
    wide = per * r
    B = lambda *s: pltpu.VMEM(s, BF16)
    cut = lambda n: (HALVES, n, wide // HALVES, nr)
    small = (sds(r, ni), sds(r, nj), sds(r, nr), sds(r * r, r))
    temp, s, lon, lat, rad, core = pl.pallas_call(
        functools.partial(sweep_kernel, nl, nz),
        out_shape=(sds(ni, nj, nr), sds(ni, r, nr)) + small,
        in_specs=[pl.BlockSpec(memory_space=pltpu.HBM)] * 6,
        out_specs=(pl.BlockSpec(memory_space=pl.ANY),) + (vm,) * 5,
        scratch_shapes=[
            V(ni, nj, nr), V(ni, nj, nr), V(r, ni), V(r, nj), V(r, nr),
            V(ni, nj, nr), V(ni, nj, nr), V(ni + 1, nj, nr), V(ni, nj, nr), V(ni, nj, nr),
            V(2, ni, nr), V(STEPS + 1, 2, nj, nr), V(STEPS + 1, 2, ni, nr), V(STEPS + 2, 2, ni, nr),
            V(2, 5, ni, nr), V(r, ni, nj), B(r, nj, 2 * ni), V(r, nj, nr), B(r, 2 * nj, nr), V(r, r, nr),
            V(blocks, ni, 128), V(2, r, r),
            V(nl, nj, wide), V(nl, nj, wide), V(nz, r, wide),
            V(*cut(nl)), V(*cut(nl)), V(*cut(nz)), V(nl, r, wide),
            V(nz, r, ni), V(nl, r, nj), V(nl, r, nr),
            V(nl, r, r), V(nz, r, r),
            V(rows, 128), V(nl, piece, 128), V(nz, piece, 128), V(rows, 128),
            pltpu.SemaphoreType.DMA((phases, most)),
            pltpu.SemaphoreType.DMA((phases, most)),
            pltpu.SemaphoreType.DMA((STEPS + 1, 4)),
            pltpu.SemaphoreType.DMA((STEPS + 1, 4)),
            pltpu.SemaphoreType.DMA,
            pltpu.SemaphoreType.DMA((6, 4)),
        ],
        compiler_params=pltpu.CompilerParams(
            collective_id=1, has_side_effects=True, vmem_limit_bytes=48 * 1024 * 1024
        ),
    )(*(pltpu.with_memory_space_constraint(x, pltpu.HBM) for x in (t, k, q, u.T, v.T, w.T)))
    anywhere = pl.BlockSpec(memory_space=pl.ANY)
    temp, err, lon, lat, rad, core = pl.pallas_call(
        error_kernel,
        out_shape=(sds(ni, nj, nr), sds(ni, nj, nr)) + small,
        in_specs=[vm] * 6,
        out_specs=(anywhere, anywhere) + (vm,) * 4,
        scratch_shapes=[
            V(ni, nj, nr), pltpu.SemaphoreType.DMA((ni // 8,)), pltpu.SemaphoreType.DMA
        ],
        compiler_params=pltpu.CompilerParams(vmem_limit_bytes=12 * 1024 * 1024),
    )(temp, s, lon, lat, rad, core)
    return temp, err, lon.T, lat.T, rad.T, core.reshape(r, r, r)


def solution(mesh):
    grid = P("lon", "lat", None)
    in_specs = (grid, grid, grid, P("lon", None), P("lat", None), P())
    out_specs = (grid, grid, P("lon", None), P("lat", None), P(), P())
    return jax.shard_map(local, mesh=mesh, in_specs=in_specs, out_specs=out_specs, check_vma=False)
```

```python
import functools

import jax
import jax.numpy as jnp
from jax import lax
from jax.experimental import pallas as pl
from jax.experimental.pallas import tpu as pltpu
from jax.sharding import PartitionSpec as P

STEPS = 4
time_step = 0.15
F32 = jnp.float32
BF16 = jnp.bfloat16
UNROLL = 6
PARTS = 2
BEFORE = (0.0, 0.5, 0.7, 1.0)
CUT = 32
NN = (((1,), (0,)), ((), ()))
NT = (((1,), (1,)), ((), ()))
TN = (((0,), (0,)), ((), ()))


def split(x):
    hi = x.astype(BF16)
    return hi, (x - hi.astype(F32)).astype(BF16)


def dot3(a, b, dims=NN):
    ah, al = a
    bh, bl = b
    d = functools.partial(lax.dot_general, dimension_numbers=dims, preferred_element_type=F32)
    return d(ah, bh) + d(ah, bl) + d(al, bh)


def mm(a, b, dims=NN):
    return dot3(split(a), split(b), dims)


def mmh(a, b, dims=NN):
    return lax.dot_general(
        a, b, dims, precision=lax.Precision.HIGHEST, preferred_element_type=F32
    )


def reciprocal(x):
    guess = pltpu.reciprocal(x, approx=True)
    return guess * (2.0 - x * guess)


def chol_inverse(gram):
    n = gram.shape[0]
    row = lax.broadcasted_iota(jnp.int32, (n, n), 0)
    col = lax.broadcasted_iota(jnp.int32, (n, n), 1)
    eye = jnp.where(row == col, 1.0, 0.0).astype(F32)
    m = jnp.concatenate([gram, eye], axis=1)
    rows = lax.broadcasted_iota(jnp.int32, m.shape, 0)
    for k in range(0, n, 2):
        first = jnp.broadcast_to(m[:, k : k + 1], m.shape)
        second = jnp.broadcast_to(m[:, k + 1 : k + 2], m.shape)
        top = m[k : k + 1, :]
        inverse = reciprocal(first[k : k + 1, :])
        ratio = first[k + 1 : k + 2, :] * inverse
        nxt = m[k + 1 : k + 2, :] - ratio * top
        if k + 2 < n:
            pivot = second[k + 1 : k + 2, :] - ratio * first[k + 1 : k + 2, :]
            update = first * inverse * top + (second - ratio * first) * reciprocal(pivot) * nxt
            m = jnp.where(rows > k + 1, m - update, jnp.where(rows == k + 1, nxt, m))
        else:
            m = jnp.where(rows == k + 1, nxt, m)
    diag = jnp.sum(jnp.where(row == col, m[:, :n], 0.0), axis=1, keepdims=True)
    return m[:, n:] / jnp.sqrt(diag)


def block_diag(x, count):
    n = x.shape[0]
    wide = jnp.concatenate([x] * count, axis=1)
    full = jnp.concatenate([wide] * count, axis=0)
    row = lax.broadcasted_iota(jnp.int32, full.shape, 0) // n
    col = lax.broadcasted_iota(jnp.int32, full.shape, 1) // n
    return jnp.where(row == col, full, 0.0)


class Comm:
    def __init__(self, nl, nz, send_sem, recv_sem, halo_send, halo_recv):
        self.halo_send, self.halo_recv = halo_send, halo_recv
        self.nl, self.nz = nl, nz
        self.lon = lax.axis_index("lon")
        self.lat = lax.axis_index("lat")
        self.send_sem, self.recv_sem = send_sem, recv_sem
        self.phase = 0
        self.sent = []

    def start(self, axis, source, target):
        count = self.nl if axis == "lon" else self.nz
        me = self.lon if axis == "lon" else self.lat
        ph = self.phase
        self.phase += 1
        waits = []
        for d in range(1, count):
            peer = lax.rem(me + d, count)
            owner = lax.rem(me + count - d, count)
            copy = pltpu.make_async_remote_copy(
                src_ref=source(peer),
                dst_ref=target(me),
                send_sem=self.send_sem.at[ph, d],
                recv_sem=self.recv_sem.at[ph, d],
                device_id={axis: peer},
                device_id_type=pl.DeviceIdType.MESH,
            )
            copy.start()
            self.sent.append(copy)
            waits.append(
                pltpu.make_async_remote_copy(
                    src_ref=target(owner),
                    dst_ref=target(owner),
                    send_sem=self.send_sem.at[ph, d],
                    recv_sem=self.recv_sem.at[ph, d],
                    device_id={axis: peer},
                    device_id_type=pl.DeviceIdType.MESH,
                )
            )
        return waits

    def scatter(self, axis, make, source, target):
        count = self.nl if axis == "lon" else self.nz
        me = self.lon if axis == "lon" else self.lat
        ph = self.phase
        self.phase += 1
        waits = []
        for d in range(1, count):
            peer = lax.rem(me + d, count)
            owner = lax.rem(me + count - d, count)
            source[peer] = make(peer)
            ends = dict(
                send_sem=self.send_sem.at[ph, d],
                recv_sem=self.recv_sem.at[ph, d],
                device_id={axis: peer},
                device_id_type=pl.DeviceIdType.MESH,
            )
            copy = pltpu.make_async_remote_copy(
                src_ref=source.at[peer], dst_ref=target.at[me], **ends
            )
            copy.start()
            self.sent.append(copy)
            waits.append(pltpu.make_async_remote_copy(
                src_ref=target.at[owner], dst_ref=target.at[owner], **ends
            ))
        target[me] = make(me)
        return waits

    def send(self, axis, shift, k, lane, source, target):
        count = self.nl if axis == "lon" else self.nz
        me = self.lon if axis == "lon" else self.lat
        return pltpu.make_async_remote_copy(
            src_ref=source,
            dst_ref=target,
            send_sem=self.halo_send.at[k, lane],
            recv_sem=self.halo_recv.at[k, lane],
            device_id={axis: lax.rem(me + shift + count, count)},
            device_id_type=pl.DeviceIdType.MESH,
        )

    def gather(self, axis, slots):
        me = self.lon if axis == "lon" else self.lat
        return self.start(axis, lambda peer: slots.at[me], lambda owner: slots.at[owner])

    def wait(self, waits):
        for w in waits:
            w.wait_recv()

    def finish(self):
        for c in self.sent:
            c.wait_send()


def total(slots):
    out = slots[0]
    for k in range(1, slots.shape[0]):
        out = out + slots[k]
    return out


def finish_reduce(comm, first, rs, zs, ag, during):
    rows = rs.shape[1]
    piece = lambda ref, p: ref.at[pl.ds(pl.multiple_of(p * rows, rows), rows)]
    during[0]()
    comm.wait(first)
    zs[comm.lat] = total(rs)
    second = comm.gather("lat", zs)
    during[1]()
    comm.wait(second)
    piece(ag, comm.lon)[...] = total(zs)
    third = comm.start("lon", lambda peer: piece(ag, comm.lon), lambda owner: piece(ag, owner))
    during[2]()
    comm.wait(third)


def reciprocal(x):
    guess = pltpu.reciprocal(x, approx=True)
    return guess * (2.0 - x * guess)


def chol_inverse(gram):
    n = gram.shape[0]
    row = lax.broadcasted_iota(jnp.int32, (n, n), 0)
    col = lax.broadcasted_iota(jnp.int32, (n, n), 1)
    eye = jnp.where(row == col, 1.0, 0.0).astype(F32)
    m = jnp.concatenate([gram, eye], axis=1)
    rows = lax.broadcasted_iota(jnp.int32, m.shape, 0)
    for k in range(0, n, 2):
        first = jnp.broadcast_to(m[:, k : k + 1], m.shape)
        second = jnp.broadcast_to(m[:, k + 1 : k + 2], m.shape)
        top = m[k : k + 1, :]
        inverse = reciprocal(first[k : k + 1, :])
        ratio = first[k + 1 : k + 2, :] * inverse
        nxt = m[k + 1 : k + 2, :] - ratio * top
        if k + 2 < n:
            pivot = second[k + 1 : k + 2, :] - ratio * first[k + 1 : k + 2, :]
            update = first * inverse * top + (second - ratio * first) * reciprocal(pivot) * nxt
            m = jnp.where(rows > k + 1, m - update, jnp.where(rows == k + 1, nxt, m))
        else:
            m = jnp.where(rows == k + 1, nxt, m)
    diag = jnp.sum(jnp.where(row == col, m[:, :n], 0.0), axis=1, keepdims=True)
    return m[:, n:] / jnp.sqrt(diag)


def block_diag(x, count):
    n = x.shape[0]
    wide = jnp.concatenate([x] * count, axis=1)
    full = jnp.concatenate([wide] * count, axis=0)
    row = lax.broadcasted_iota(jnp.int32, full.shape, 0) // n
    col = lax.broadcasted_iota(jnp.int32, full.shape, 1) // n
    return jnp.where(row == col, full, 0.0)


class Comm:
    def __init__(self, nl, nz, send_sem, recv_sem, halo_send, halo_recv):
        self.halo_send, self.halo_recv = halo_send, halo_recv
        self.nl, self.nz = nl, nz
        self.lon = lax.axis_index("lon")
        self.lat = lax.axis_index("lat")
        self.send_sem, self.recv_sem = send_sem, recv_sem
        self.phase = 0
        self.sent = []

    def start(self, axis, source, target):
        count = self.nl if axis == "lon" else self.nz
        me = self.lon if axis == "lon" else self.lat
        ph = self.phase
        self.phase += 1
        waits = []
        for d in range(1, count):
            peer = lax.rem(me + d, count)
            owner = lax.rem(me + count - d, count)
            copy = pltpu.make_async_remote_copy(
                src_ref=source(peer),
                dst_ref=target(me),
                send_sem=self.send_sem.at[ph, d],
                recv_sem=self.recv_sem.at[ph, d],
                device_id={axis: peer},
                device_id_type=pl.DeviceIdType.MESH,
            )
            copy.start()
            self.sent.append(copy)
            waits.append(
                pltpu.make_async_remote_copy(
                    src_ref=target(owner),
                    dst_ref=target(owner),
                    send_sem=self.send_sem.at[ph, d],
                    recv_sem=self.recv_sem.at[ph, d],
                    device_id={axis: peer},
                    device_id_type=pl.DeviceIdType.MESH,
                )
            )
        return waits

    def scatter(self, axis, make, source, target):
        count = self.nl if axis == "lon" else self.nz
        me = self.lon if axis == "lon" else self.lat
        ph = self.phase
        self.phase += 1
        waits = []
        for d in range(1, count):
            peer = lax.rem(me + d, count)
            owner = lax.rem(me + count - d, count)
            source[peer] = make(peer)
            ends = dict(
                send_sem=self.send_sem.at[ph, d],
                recv_sem=self.recv_sem.at[ph, d],
                device_id={axis: peer},
                device_id_type=pl.DeviceIdType.MESH,
            )
            copy = pltpu.make_async_remote_copy(
                src_ref=source.at[peer], dst_ref=target.at[me], **ends
            )
            copy.start()
            self.sent.append(copy)
            waits.append(pltpu.make_async_remote_copy(
                src_ref=target.at[owner], dst_ref=target.at[owner], **ends
            ))
        target[me] = make(me)
        return waits

    def send(self, axis, shift, k, lane, source, target):
        count = self.nl if axis == "lon" else self.nz
        me = self.lon if axis == "lon" else self.lat
        return pltpu.make_async_remote_copy(
            src_ref=source,
            dst_ref=target,
            send_sem=self.halo_send.at[k, lane],
            recv_sem=self.halo_recv.at[k, lane],
            device_id={axis: lax.rem(me + shift + count, count)},
            device_id_type=pl.DeviceIdType.MESH,
        )

    def gather(self, axis, slots):
        me = self.lon if axis == "lon" else self.lat
        return self.start(axis, lambda peer: slots.at[me], lambda owner: slots.at[owner])

    def wait(self, waits):
        for w in waits:
            w.wait_recv()

    def finish(self):
        for c in self.sent:
            c.wait_send()


def total(slots):
    out = slots[0]
    for k in range(1, slots.shape[0]):
        out = out + slots[k]
    return out


def all_reduce(comm, buf, rs, zs, ag, during=None):
    rows = rs.shape[1]
    piece = lambda ref, p: ref.at[pl.ds(pl.multiple_of(p * rows, rows), rows)]
    first = comm.start("lon", lambda peer: piece(buf, peer), lambda owner: rs.at[owner])
    rs[comm.lon] = piece(buf, comm.lon)[...]
    if during is not None:
        during[0]()
    comm.wait(first)
    zs[comm.lat] = total(rs)
    second = comm.gather("lat", zs)
    if during is not None:
        during[1]()
    comm.wait(second)
    piece(ag, comm.lon)[...] = total(zs)
    third = comm.start("lon", lambda peer: piece(ag, comm.lon), lambda owner: piece(ag, owner))
    if during is not None:
        during[2]()
    comm.wait(third)


def harmonic(cond_a, cond_b):
    summed = cond_a + cond_b
    safe = jnp.where(summed > 0.0, summed, 1.0)
    guess = pltpu.reciprocal(safe, approx=True)
    guess = guess * (2.0 - safe * guess)
    return (cond_a + cond_a) * cond_b * guess


def in_groups(low, high, size, group):
    trips = (high - low) // size

    @pl.loop(0, trips)
    def _(trip):
        group(low + trip * size, size)

    left = max(high - low, 0) - trips * size
    if left:
        group(high - left, left)


def batched(low, high, size, values, store):
    def group(first, count):
        outs = [values(first + k) for k in range(count)]
        for k, out in enumerate(outs):
            store(first + k, out)

    in_groups(low, high, size, group)


def store_in(ref):
    def store(i, value):
        ref[i] = value

    return store


def conduct(comm, t0, k_ref, q_ref, ta, tb, hx, hy, hz, edge_k, hal_lon, hal_lat, pack, plane, wait_q):
    ni, nj, nr = t0.shape
    last = STEPS
    has_lo, has_hi = comm.lat > 0, comm.lat < comm.nz - 1
    sides = ((0, 0, 1), (1, nj - 1, nj - 2))

    def exchange_lat(k):
        copies = (
            (has_hi, has_lo, comm.send("lat", 1, k, 2, pack.at[k, 1], hal_lat.at[k, 0])),
            (has_lo, has_hi, comm.send("lat", -1, k, 3, pack.at[k, 0], hal_lat.at[k, 1])),
        )
        for out, _, c in copies:
            pl.when(out)(c.start)
        return copies

    def exchange_lon(k, src):
        copies = (
            comm.send("lon", 1, k, 0, src.at[ni - 1], hal_lon.at[k, 0]),
            comm.send("lon", -1, k, 1, src.at[0], hal_lon.at[k, 1]),
        )
        for c in copies:
            c.start()
        return copies

    def wait(lat_copies, lon_copies):
        for c in lon_copies:
            c.wait_recv()
        for _, into, c in lat_copies:
            pl.when(into)(c.wait_recv)

    def wait_sent(lat_copies, lon_copies):
        for c in lon_copies:
            c.wait_send()
        for out, _, c in lat_copies:
            pl.when(out)(c.wait_send)

    for side, j, _ in sides:
        pack[last, side] = k_ref[:, j, :]
        pack[0, side] = t0[:, j, :]
    sent_k = exchange_lat(last), exchange_lon(last, k_ref)
    sent_t = exchange_lat(0), exchange_lon(0, t0)

    @pl.when(comm.lat == 0)
    def _():
        for k in range(STEPS + 1):
            hal_lat[k, 0] = jnp.zeros((ni, nr), F32)

    @pl.when(comm.lat == comm.nz - 1)
    def _():
        for k in range(STEPS + 1):
            hal_lat[k, 1] = jnp.zeros((ni, nr), F32)

    row = lax.broadcasted_iota(jnp.int32, (nj, nr), 0)
    col = lax.broadcasted_iota(jnp.int32, (nj, nr), 1)
    plane_row = lax.broadcasted_iota(jnp.int32, (ni, nr), 0)

    def faces(i):
        k = k_ref[i]
        return (
            jnp.where(row == 0, 0.0, harmonic(k, pltpu.roll(k, 1, 0))),
            jnp.where(col == 0, 0.0, harmonic(k, pltpu.roll(k, 1, 1))),
        )

    def store_faces(i, values):
        hy[i], hz[i] = values

    batched(0, ni, 2, faces, store_faces)
    batched(1, ni, 4, lambda i: harmonic(k_ref[i], k_ref[i - 1]), store_in(hx))
    wait_q()
    wait(*sent_k)
    hx[0] = harmonic(k_ref[0], hal_lon[last, 0])
    hx[ni] = harmonic(k_ref[ni - 1], hal_lon[last, 1])
    for side, j, inner in sides:
        edge_k[side] = harmonic(pack[last, side], hal_lat[last, side])
        plane[side, 0] = q_ref[:, j, :]
        plane[side, 1] = hx[pl.ds(0, ni), j, :]
        plane[side, 2] = hx[pl.ds(1, ni), j, :]
        plane[side, 3] = hy[:, max(j, inner), :]
        plane[side, 4] = hz[:, j, :]

    def radial(h, here):
        flux = h * (here - pltpu.roll(here, 1, 1))
        return pltpu.roll(flux, nr - 1, 1) - flux

    def slab(i, here, before_flux, after_flux):
        fy = hy[i] * (here - pltpu.roll(here, 1, 0))
        change = q_ref[i] + (after_flux - before_flux)
        change = change + (pltpu.roll(fy, nj - 1, 0) - fy) + radial(hz[i], here)
        return here + time_step * change

    buffers = lambda step: (t0 if step == 0 else (ta, tb)[(step - 1) % 2], (ta, tb)[step % 2])
    slot = lambda step: step + (step >= last)

    def inside(step, low, high):
        src, dst = buffers(step)

        def group(first, count):
            cells = [src[first - 1 + n] for n in range(count + 2)]
            fluxes = [hx[first + n] * (cells[n + 1] - cells[n]) for n in range(count + 1)]
            outs = [slab(first + n, cells[n + 1], fluxes[n], fluxes[n + 1]) for n in range(count)]
            for n, out in enumerate(outs):
                dst[first + n] = out

        in_groups(low, high, UNROLL, group)

    def edges(step, more):
        src, dst = buffers(step)
        for side, j, inner in sides:
            here = pack[step, side]
            before = jnp.where(plane_row == 0, hal_lon[step, 0, pl.ds(j, 1), :], pltpu.roll(here, 1, 0))
            after = jnp.where(plane_row == ni - 1, hal_lon[step, 1, pl.ds(j, 1), :], pltpu.roll(here, ni - 1, 0))
            change = plane[side, 0] + plane[side, 2] * (after - here) - plane[side, 1] * (here - before)
            change = change + plane[side, 3] * (src[:, inner, :] - here)
            change = change + edge_k[side] * (hal_lat[step, side] - here) + radial(plane[side, 4], here)
            pack[slot(step + 1), side] = here + time_step * change
        lat_copies = exchange_lat(step + 1) if more else ()
        for i, before, after in (
            (0, hal_lon[step, 0], src[1]), (ni - 1, src[ni - 2], hal_lon[step, 1])
        ):
            here = src[i]
            dst[i] = slab(i, here, hx[i] * (here - before), hx[i + 1] * (after - here))
            for side, j, _ in sides:
                dst[i, pl.ds(j, 1), :] = pack[slot(step + 1), side, pl.ds(i, 1), :]
        lon_copies = exchange_lon(step + 1, dst) if more else ()
        return lat_copies, lon_copies

    def seam(step):
        dst = buffers(step)[1]
        for side, j, _ in sides:
            dst[pl.ds(1, ni - 2), j, :] = pack[slot(step + 1), side, pl.ds(1, ni - 2), :]

    for step in range(STEPS):
        middle = 1 + UNROLL * int((ni - 2) // UNROLL * BEFORE[step])
        if step == STEPS - 1:
            middle = ni - 1
        inside(step, 1, middle)
        wait(*sent_t)
        going = edges(step, step < STEPS - 1)
        inside(step, middle, ni - 1)
        seam(step)
        wait_sent(*sent_t)
        sent_t = going
    wait_sent(*sent_k)


def stacked(x, axis):
    n = x.shape[axis]
    both = jnp.concatenate([x, x], axis=axis)
    low = both - both.astype(BF16).astype(F32)
    return jnp.where(lax.broadcasted_iota(jnp.int32, both.shape, axis) < n, both, low).astype(BF16)


def left_operand(x):
    high, low = split(jnp.concatenate([x, x], axis=1))
    col = lax.broadcasted_iota(jnp.int32, low.shape, 1)
    low = jnp.where(col < x.shape[1], low.astype(F32), 0.0).astype(BF16)
    return jnp.concatenate([high, low], axis=0)


def fold_rows(x):
    n = x.shape[0] // 2
    return x[:n] + x[n:]


def dot1(a, b, dims=NN):
    return lax.dot_general(a, b, dims, preferred_element_type=F32)


def sweep_kernel(nl, nz, t_in, k_in, q_in, u_in, v_in, w_in,
                 temp_ref, x3, lon_ref, lat_ref, rad_ref, core_ref,
                 k_ref, q_ref, u_ref, v_ref, w_ref,
                 ta, tb, hx, hy, hz, edge_k, hal_lon, hal_lat, pack, plane,
                 z1, z1t, xs, xh, f_ref, yx, small,
                 y2s, y2r, p2z, y3s, y3r, y3z, us,
                 b1s, b2s, b3s, g1s, g2s, buf, rs, zs, ag,
                 send_sem, recv_sem, halo_send, halo_recv, out_sem, in_sem):
    comm = Comm(nl, nz, send_sem, recv_sem, halo_send, halo_recv)
    t0 = tb
    ni, nj, nr = t0.shape
    t_ref = (ta, tb)[(STEPS - 1) % 2]
    r = u_ref.shape[0]
    group = 128 // r
    blocks = r // group
    per = r // nl
    wide = per * r

    fetches = {}
    for n, (source, target) in enumerate((
        (t_in, t0), (k_in, k_ref), (q_in, q_ref), (u_in, u_ref), (v_in, v_ref), (w_in, w_ref)
    )):
        fetches[n] = [pltpu.make_async_copy(source, target, in_sem.at[n, 0])]
        if n < 3:
            part = ni // 4
            fetches[n] = [
                pltpu.make_async_copy(
                    source.at[pl.ds(part * c, part)], target.at[pl.ds(part * c, part)], in_sem.at[n, c]
                )
                for c in range(4)
            ]

    def fetched(*wanted):
        for n in wanted:
            for c in fetches[n]:
                c.wait()

    barrier = pltpu.get_barrier_semaphore()
    for d in range(1, nl):
        pl.semaphore_signal(barrier, inc=1, device_id={"lon": lax.rem(comm.lon + d, nl)},
                            device_id_type=pl.DeviceIdType.MESH)
    for d in range(1, nz):
        pl.semaphore_signal(barrier, inc=1, device_id={"lat": lax.rem(comm.lat + d, nz)},
                            device_id_type=pl.DeviceIdType.MESH)
    for n in (1, 0, 2, 3, 4, 5):
        for c in fetches[n]:
            c.start()
    fetched(1, 0)

    pl.semaphore_wait(barrier, nl + nz - 2)
    conduct(comm, t0, k_ref, q_ref, ta, tb, hx, hy, hz, edge_k, hal_lon, hal_lat, pack, plane,
            lambda: fetched(2, 3, 4, 5))
    out_copy = pltpu.make_async_copy(t_ref, temp_ref, out_sem)
    out_copy.start()

    wts = split(w_ref[...])
    ut = u_ref[...]
    vt = v_ref[...]
    low_i = ni // 2
    wx = left_operand(w_ref[...])
    join = lambda x: jnp.concatenate(split(x), axis=1)

    def contract_rad(first, count):
        outs = []
        for k in range(0, count, 2):
            cells = [t_ref[first + k + e + h * low_i] for e in range(2) for h in range(2)]
            cells = jnp.concatenate([join(x) for x in cells], axis=0)
            outs.append(fold_rows(dot1(wx, cells, NT)))
        for n, out in enumerate(outs):
            z1[:, first + 2 * n, :] = out[:, : 2 * nj]
            z1[:, first + 2 * n + 1, :] = out[:, 2 * nj :]

    in_groups(0, low_i, 4, contract_rad)

    lane = lambda n, w: lax.rem(lax.broadcasted_iota(jnp.int32, (n, w), 1), 128) // r
    v4h, v4l = split(jnp.concatenate([vt.T] * group, axis=1))
    none = jnp.zeros_like(v4h)
    beside = lambda x: jnp.concatenate(
        [jnp.concatenate([x, none], axis=1), jnp.concatenate([none, x], axis=1)], axis=0
    )
    vhigh = jnp.concatenate([beside(v4h)] * 2, axis=0)
    vlow = beside(v4l)
    ux = left_operand(ut)

    def y1block(m):
        cells = jnp.concatenate([join(z1[m * group + g]) for g in range(group)], axis=0)
        both = dot1(cells, vhigh) + dot1(cells[:, : 2 * nj], vlow)
        out = both[:low_i]
        for g in range(1, group):
            out = jnp.where(lane(low_i, 256) == g, both[g * low_i : (g + 1) * low_i], out)
        out = jnp.concatenate([out[:, :128], out[:, 128:]], axis=0)
        yx[m] = join(out)
        return fold_rows(dot1(ux, stacked(out, 0)))

    if rs.shape[1] == r:
        first = comm.scatter("lon", y1block, buf, rs)
    else:
        for m in range(blocks):
            block = y1block(m)
            for c in range(r // rs.shape[1]):
                buf[m * (r // rs.shape[1]) + c] = block[c * rs.shape[1] : (c + 1) * rs.shape[1]]
        rs[comm.lon] = buf[comm.lon]
        first = comm.start("lon", lambda peer: buf.at[peer], lambda owner: rs.at[owner])

    def turn(low, high):
        for b in range(low, high):
            cell = z1[b]
            z1t[b] = stacked(jnp.concatenate([cell[:, :nj], cell[:, nj:]], axis=0).T, 1)

    turns = tuple(functools.partial(turn, r * k // 3, r * (k + 1) // 3) for k in range(3))
    finish_reduce(comm, first, rs, zs, ag, turns)

    acc = jnp.zeros((2 * r, ni), F32)
    for m in range(blocks):
        acc = acc + dot1(left_operand(ag[pl.ds(m * r, r), :]), yx[m], NT)
    acc = fold_rows(acc)
    b1s[comm.lat] = acc
    w = comm.gather("lat", b1s)
    comm.wait(w)
    b1t = total(b1s)
    g1s[comm.lon] = mmh(b1t, b1t, NT)
    g1w = comm.gather("lon", g1s)

    bh, bl = split(jnp.concatenate([b1t] * per, axis=0).T)
    b1x = jnp.concatenate([
        jnp.concatenate([bh, bh], axis=0),
        jnp.concatenate([bl, jnp.zeros_like(bl)], axis=0),
    ], axis=1)

    def y2piece(p):
        out = jnp.zeros((nj, wide), F32)
        for g in range(per):
            both = dot1(z1t[p * per + g], b1x)
            out = jnp.where(lane(nj, wide) == g, both[:, :wide] + both[:, wide:], out)
        return out

    w = comm.scatter("lon", y2piece, y2s, y2r)
    comm.wait(w)
    y2 = split(total(y2r))
    p2z[comm.lat] = dot3(split(vt), y2)
    w = comm.gather("lat", p2z)
    comm.wait(g1w)
    small[0] = chol_inverse(total(g1s))
    l1 = small[0]
    bd1 = split(block_diag(mmh(l1, l1, TN), per))
    lont = mmh(l1, b1t)
    lon_ref[...] = lont
    lonx = left_operand(lont)

    def contract_lon(low, high):
        for j in range(low, high, 2):
            pair = jnp.concatenate(
                [stacked(t_ref[:, j, :], 0), stacked(t_ref[:, j + 1, :], 0)], axis=1
            )
            out = fold_rows(dot1(lonx, pair))
            xs[:, j, :] = out[:, :nr]
            xs[:, j + 1, :] = out[:, nr:]

    contract_lon(0, CUT)
    comm.wait(w)
    b2s[comm.lon] = dot3(split(dot3(split(total(p2z)), bd1)), y2, NT)
    w = comm.gather("lon", b2s)
    contract_lon(CUT, nj)
    for a in range(r):
        xh[a] = stacked(xs[a], 0)
    comm.wait(w)
    b2t = total(b2s)
    g2s[comm.lat] = mmh(b2t, b2t, NT)
    g2w = comm.gather("lat", g2s)
    b2x = left_operand(b2t)
    parts = y3s.shape[0]
    half = per // parts

    def y3piece(h, p):
        outs = []
        first = p * per + h * half
        for g in range(0, half, 2):
            mates = [xh[first + k] for k in range(g, min(g + 2, half))]
            out = fold_rows(dot1(b2x, jnp.concatenate(mates, axis=1)))
            outs += [out[:, nr * k : nr * (k + 1)] for k in range(len(mates))]
        return jnp.concatenate(outs, axis=0)

    ws = [
        comm.scatter("lon", functools.partial(y3piece, h), y3s.at[h], y3r.at[h])
        for h in range(parts)
    ]
    for h in range(parts):
        comm.wait(ws[h])
        y3z[h, comm.lat] = total(y3r.at[h])
        ws[h] = comm.gather("lat", y3z.at[h])
    comm.wait(g2w)
    small[1] = chol_inverse(total(g2s))
    l2 = small[1]
    bd2 = split(block_diag(l2, per))
    latt = mmh(l2, b2t)
    lat_ref[...] = latt
    for w in ws:
        comm.wait(w)
    whole = jnp.concatenate([total(y3z.at[h]) for h in range(parts)], axis=0)
    y3 = split(dot3(bd2, split(whole)))
    p3 = dot3(wts, y3, NT)
    b3s[comm.lon] = dot3(split(p3), y3)
    w = comm.gather("lon", b3s)
    comm.wait(w)
    b3t = total(b3s)
    us[comm.lon] = dot3(split(b3t), y3, NT)
    w = comm.gather("lon", us)
    small[0] = chol_inverse(mmh(b3t, b3t, NT))
    l3 = small[0]
    radt = mmh(l3, b3t)
    rad_ref[...] = radt
    back_high, back_low = split(mmh(l3, radt, TN))
    back = jnp.concatenate([back_high, back_high, back_low], axis=0)
    l3h = split(l3)
    lonb = left_operand(lont.T)
    comm.wait(w)
    for p in range(nl):
        high, low = split(us[p])
        cells = jnp.concatenate([high, low, high], axis=0)
        f_ref[pl.ds(p * per, per)] = dot1(cells, back, TN).reshape(per, r, nr)
    for b in range(0, r, 2):
        pair = jnp.concatenate([stacked(f_ref[:, b + e, :], 0) for e in range(2)], axis=1)
        out = fold_rows(dot1(lonb, pair))
        x3[:, b, :] = out[:, :nr]
        x3[:, b + 1, :] = out[:, nr:]
    for p in range(nl):
        core_ref[pl.ds(p * wide, wide), :] = dot3(l3h, split(us[p])).T
    out_copy.wait()
    comm.finish()


def error_kernel(t_ref, s_ref, lon_ref, lat_ref, rad_ref, core_ref,
                 temp_out, err_out, lon_out, lat_out, rad_out, core_out, err, sem, temp_sem):
    temp_copy = pltpu.make_async_copy(t_ref, temp_out, temp_sem)
    temp_copy.start()
    latx = left_operand(lat_ref[...].T)
    ni, _, nr = t_ref.shape
    at = 16

    def chunk(c):
        part = pl.ds(c * at, at)
        return pltpu.make_async_copy(err.at[part], err_out.at[part], sem.at[c])

    @pl.loop(0, ni // at)
    def _(c):
        outs = []
        for k in range(0, at, 2):
            mates = [stacked(s_ref[c * at + k + e], 0) for e in range(2)]
            both = fold_rows(dot1(latx, jnp.concatenate(mates, axis=1)))
            outs += [both[:, :nr], both[:, nr:]]
        for k, out in enumerate(outs):
            err[c * at + k] = t_ref[c * at + k] - out
        chunk(c).start()

    lon_out[...] = lon_ref[...]
    lat_out[...] = lat_ref[...]
    rad_out[...] = rad_ref[...]
    core_out[...] = core_ref[...]

    @pl.loop(0, ni // at)
    def _(c):
        chunk(c).wait()

    temp_copy.wait()


def local(t, k, q, u, v, w):
    nl, nz = lax.axis_size("lon"), lax.axis_size("lat")
    ni, nj, nr = t.shape
    r = u.shape[1]
    rows = r * r * r // 128
    piece = rows // nl
    blocks = r * r // 128
    most = max(nl, nz)
    vm = pl.BlockSpec(memory_space=pltpu.VMEM)
    sds = lambda *s: jax.ShapeDtypeStruct(s, F32)
    V = lambda *s: pltpu.VMEM(s, F32)
    phases = 11 + 2 * PARTS
    per = r // nl
    wide = per * r
    B = lambda *s: pltpu.VMEM(s, BF16)
    parts = min(PARTS, per)
    cut = lambda n: (parts, n, wide // parts, nr)
    small = (sds(r, ni), sds(r, nj), sds(r, nr), sds(r * r, r))
    temp, s, lon, lat, rad, core = pl.pallas_call(
        functools.partial(sweep_kernel, nl, nz),
        out_shape=(sds(ni, nj, nr), sds(ni, r, nr)) + small,
        in_specs=[pl.BlockSpec(memory_space=pltpu.HBM)] * 6,
        out_specs=(pl.BlockSpec(memory_space=pl.ANY),) + (vm,) * 5,
        scratch_shapes=[
            V(ni, nj, nr), V(ni, nj, nr), V(r, ni), V(r, nj), V(r, nr),
            V(ni, nj, nr), V(ni, nj, nr), V(ni + 1, nj, nr), V(ni, nj, nr), V(ni, nj, nr),
            V(2, ni, nr), V(STEPS + 1, 2, nj, nr), V(STEPS + 1, 2, ni, nr), V(STEPS + 2, 2, ni, nr),
            V(2, 5, ni, nr), V(r, ni // 2, 2 * nj), B(r, nj, 2 * ni), V(r, nj, nr), B(r, 2 * nj, nr), V(r, r, nr),
            B(blocks, ni, 256), V(2, r, r),
            V(nl, nj, wide), V(nl, nj, wide), V(nz, r, wide),
            V(*cut(nl)), V(*cut(nl)), V(*cut(nz)), V(nl, r, wide),
            V(nz, r, ni), V(nl, r, nj), V(nl, r, nr),
            V(nl, r, r), V(nz, r, r),
            V(nl, piece, 128), V(nl, piece, 128), V(nz, piece, 128), V(rows, 128),
            pltpu.SemaphoreType.DMA((phases, most)),
            pltpu.SemaphoreType.DMA((phases, most)),
            pltpu.SemaphoreType.DMA((STEPS + 1, 4)),
            pltpu.SemaphoreType.DMA((STEPS + 1, 4)),
            pltpu.SemaphoreType.DMA,
            pltpu.SemaphoreType.DMA((6, 4)),
        ],
        compiler_params=pltpu.CompilerParams(
            collective_id=1, has_side_effects=True, vmem_limit_bytes=48 * 1024 * 1024
        ),
    )(*(pltpu.with_memory_space_constraint(x, pltpu.HBM) for x in (t, k, q, u.T, v.T, w.T)))
    anywhere = pl.BlockSpec(memory_space=pl.ANY)
    temp, err, lon, lat, rad, core = pl.pallas_call(
        error_kernel,
        out_shape=(sds(ni, nj, nr), sds(ni, nj, nr)) + small,
        in_specs=[vm] * 6,
        out_specs=(anywhere, anywhere) + (vm,) * 4,
        scratch_shapes=[
            V(ni, nj, nr), pltpu.SemaphoreType.DMA((ni // 16,)), pltpu.SemaphoreType.DMA
        ],
        compiler_params=pltpu.CompilerParams(vmem_limit_bytes=12 * 1024 * 1024),
    )(temp, s, lon, lat, rad, core)
    return temp, err, lon.T, lat.T, rad.T, core.reshape(r, r, r)


def solution(mesh):
    grid = P("lon", "lat", None)
    in_specs = (grid, grid, grid, P("lon", None), P("lat", None), P())
    out_specs = (grid, grid, P("lon", None), P("lat", None), P(), P())
    return jax.shard_map(local, mesh=mesh, in_specs=in_specs, out_specs=out_specs, check_vma=False)
```

```python
import functools

import jax
import jax.numpy as jnp
from jax import lax
from jax.experimental import pallas as pl
from jax.experimental.pallas import tpu as pltpu
from jax.sharding import PartitionSpec as P

STEPS = 4
time_step = 0.15
F32 = jnp.float32
BF16 = jnp.bfloat16
UNROLL = 6
PARTS = 2
BEFORE = (0.0, 0.5, 0.7, 1.0)
CUT = 32
NN = (((1,), (0,)), ((), ()))
NT = (((1,), (1,)), ((), ()))
TN = (((0,), (0,)), ((), ()))


def split(x):
    hi = x.astype(BF16)
    return hi, (x - hi.astype(F32)).astype(BF16)


def dot3(a, b, dims=NN):
    ah, al = a
    bh, bl = b
    d = functools.partial(lax.dot_general, dimension_numbers=dims, preferred_element_type=F32)
    return d(ah, bh) + d(ah, bl) + d(al, bh)


def mm(a, b, dims=NN):
    return dot3(split(a), split(b), dims)


def mmh(a, b, dims=NN):
    return lax.dot_general(
        a, b, dims, precision=lax.Precision.HIGHEST, preferred_element_type=F32
    )


def reciprocal(x):
    guess = pltpu.reciprocal(x, approx=True)
    return guess * (2.0 - x * guess)


def chol_inverse(gram):
    n = gram.shape[0]
    row = lax.broadcasted_iota(jnp.int32, (n, n), 0)
    col = lax.broadcasted_iota(jnp.int32, (n, n), 1)
    eye = jnp.where(row == col, 1.0, 0.0).astype(F32)
    m = jnp.concatenate([gram, eye], axis=1)
    rows = lax.broadcasted_iota(jnp.int32, m.shape, 0)
    for k in range(0, n, 2):
        first = jnp.broadcast_to(m[:, k : k + 1], m.shape)
        second = jnp.broadcast_to(m[:, k + 1 : k + 2], m.shape)
        top = m[k : k + 1, :]
        inverse = reciprocal(first[k : k + 1, :])
        ratio = first[k + 1 : k + 2, :] * inverse
        nxt = m[k + 1 : k + 2, :] - ratio * top
        if k + 2 < n:
            pivot = second[k + 1 : k + 2, :] - ratio * first[k + 1 : k + 2, :]
            update = first * inverse * top + (second - ratio * first) * reciprocal(pivot) * nxt
            m = jnp.where(rows > k + 1, m - update, jnp.where(rows == k + 1, nxt, m))
        else:
            m = jnp.where(rows == k + 1, nxt, m)
    diag = jnp.sum(jnp.where(row == col, m[:, :n], 0.0), axis=1, keepdims=True)
    return m[:, n:] / jnp.sqrt(diag)


def block_diag(x, count):
    n = x.shape[0]
    wide = jnp.concatenate([x] * count, axis=1)
    full = jnp.concatenate([wide] * count, axis=0)
    row = lax.broadcasted_iota(jnp.int32, full.shape, 0) // n
    col = lax.broadcasted_iota(jnp.int32, full.shape, 1) // n
    return jnp.where(row == col, full, 0.0)


class Comm:
    def __init__(self, nl, nz, send_sem, recv_sem, halo_send, halo_recv):
        self.halo_send, self.halo_recv = halo_send, halo_recv
        self.nl, self.nz = nl, nz
        self.lon = lax.axis_index("lon")
        self.lat = lax.axis_index("lat")
        self.send_sem, self.recv_sem = send_sem, recv_sem
        self.phase = 0
        self.sent = []

    def start(self, axis, source, target):
        count = self.nl if axis == "lon" else self.nz
        me = self.lon if axis == "lon" else self.lat
        ph = self.phase
        self.phase += 1
        waits = []
        for d in range(1, count):
            peer = lax.rem(me + d, count)
            owner = lax.rem(me + count - d, count)
            copy = pltpu.make_async_remote_copy(
                src_ref=source(peer),
                dst_ref=target(me),
                send_sem=self.send_sem.at[ph, d],
                recv_sem=self.recv_sem.at[ph, d],
                device_id={axis: peer},
                device_id_type=pl.DeviceIdType.MESH,
            )
            copy.start()
            self.sent.append(copy)
            waits.append(
                pltpu.make_async_remote_copy(
                    src_ref=target(owner),
                    dst_ref=target(owner),
                    send_sem=self.send_sem.at[ph, d],
                    recv_sem=self.recv_sem.at[ph, d],
                    device_id={axis: peer},
                    device_id_type=pl.DeviceIdType.MESH,
                )
            )
        return waits

    def scatter(self, axis, make, source, target):
        count = self.nl if axis == "lon" else self.nz
        me = self.lon if axis == "lon" else self.lat
        ph = self.phase
        self.phase += 1
        waits = []
        for d in range(1, count):
            peer = lax.rem(me + d, count)
            owner = lax.rem(me + count - d, count)
            source[peer] = make(peer)
            ends = dict(
                send_sem=self.send_sem.at[ph, d],
                recv_sem=self.recv_sem.at[ph, d],
                device_id={axis: peer},
                device_id_type=pl.DeviceIdType.MESH,
            )
            copy = pltpu.make_async_remote_copy(
                src_ref=source.at[peer], dst_ref=target.at[me], **ends
            )
            copy.start()
            self.sent.append(copy)
            waits.append(pltpu.make_async_remote_copy(
                src_ref=target.at[owner], dst_ref=target.at[owner], **ends
            ))
        target[me] = make(me)
        return waits

    def send(self, axis, shift, k, lane, source, target):
        count = self.nl if axis == "lon" else self.nz
        me = self.lon if axis == "lon" else self.lat
        return pltpu.make_async_remote_copy(
            src_ref=source,
            dst_ref=target,
            send_sem=self.halo_send.at[k, lane],
            recv_sem=self.halo_recv.at[k, lane],
            device_id={axis: lax.rem(me + shift + count, count)},
            device_id_type=pl.DeviceIdType.MESH,
        )

    def gather(self, axis, slots):
        me = self.lon if axis == "lon" else self.lat
        return self.start(axis, lambda peer: slots.at[me], lambda owner: slots.at[owner])

    def wait(self, waits):
        for w in waits:
            w.wait_recv()

    def finish(self):
        for c in self.sent:
            c.wait_send()


def total(slots):
    out = slots[0]
    for k in range(1, slots.shape[0]):
        out = out + slots[k]
    return out


def finish_reduce(comm, first, rs, zs, ag, during):
    rows = rs.shape[1]
    piece = lambda ref, p: ref.at[pl.ds(pl.multiple_of(p * rows, rows), rows)]
    during[0]()
    comm.wait(first)
    zs[comm.lat] = total(rs)
    second = comm.gather("lat", zs)
    during[1]()
    comm.wait(second)
    piece(ag, comm.lon)[...] = total(zs)
    third = comm.start("lon", lambda peer: piece(ag, comm.lon), lambda owner: piece(ag, owner))
    during[2]()
    comm.wait(third)


def harmonic(cond_a, cond_b):
    summed = cond_a + cond_b
    safe = jnp.where(summed > 0.0, summed, 1.0)
    guess = pltpu.reciprocal(safe, approx=True)
    guess = guess * (2.0 - safe * guess)
    return (cond_a + cond_a) * cond_b * guess


def in_groups(low, high, size, group):
    trips = (high - low) // size

    @pl.loop(0, trips)
    def _(trip):
        group(low + trip * size, size)

    left = max(high - low, 0) - trips * size
    if left:
        group(high - left, left)


def batched(low, high, size, values, store):
    def group(first, count):
        outs = [values(first + k) for k in range(count)]
        for k, out in enumerate(outs):
            store(first + k, out)

    in_groups(low, high, size, group)


def store_in(ref):
    def store(i, value):
        ref[i] = value

    return store


def conduct(comm, t0, k_ref, q_ref, ta, tb, hx, hy, hz, edge_k, hal_lon, hal_lat, pack, plane, wait_q):
    ni, nj, nr = t0.shape
    last = STEPS
    has_lo, has_hi = comm.lat > 0, comm.lat < comm.nz - 1
    sides = ((0, 0, 1), (1, nj - 1, nj - 2))

    def exchange_lat(k):
        copies = (
            (has_hi, has_lo, comm.send("lat", 1, k, 2, pack.at[k, 1], hal_lat.at[k, 0])),
            (has_lo, has_hi, comm.send("lat", -1, k, 3, pack.at[k, 0], hal_lat.at[k, 1])),
        )
        for out, _, c in copies:
            pl.when(out)(c.start)
        return copies

    def exchange_lon(k, src):
        copies = (
            comm.send("lon", 1, k, 0, src.at[ni - 1], hal_lon.at[k, 0]),
            comm.send("lon", -1, k, 1, src.at[0], hal_lon.at[k, 1]),
        )
        for c in copies:
            c.start()
        return copies

    def wait(lat_copies, lon_copies):
        for c in lon_copies:
            c.wait_recv()
        for _, into, c in lat_copies:
            pl.when(into)(c.wait_recv)

    def wait_sent(lat_copies, lon_copies):
        for c in lon_copies:
            c.wait_send()
        for out, _, c in lat_copies:
            pl.when(out)(c.wait_send)

    for side, j, _ in sides:
        pack[last, side] = k_ref[:, j, :]
        pack[0, side] = t0[:, j, :]
    sent_k = exchange_lat(last), exchange_lon(last, k_ref)
    sent_t = exchange_lat(0), exchange_lon(0, t0)

    @pl.when(comm.lat == 0)
    def _():
        for k in range(STEPS + 1):
            hal_lat[k, 0] = jnp.zeros((ni, nr), F32)

    @pl.when(comm.lat == comm.nz - 1)
    def _():
        for k in range(STEPS + 1):
            hal_lat[k, 1] = jnp.zeros((ni, nr), F32)

    row = lax.broadcasted_iota(jnp.int32, (nj, nr), 0)
    col = lax.broadcasted_iota(jnp.int32, (nj, nr), 1)
    plane_row = lax.broadcasted_iota(jnp.int32, (ni, nr), 0)

    def faces(i):
        k = k_ref[i]
        return (
            jnp.where(row == 0, 0.0, harmonic(k, pltpu.roll(k, 1, 0))),
            jnp.where(col == 0, 0.0, harmonic(k, pltpu.roll(k, 1, 1))),
        )

    def store_faces(i, values):
        hy[i], hz[i] = values

    batched(0, ni, 2, faces, store_faces)
    batched(1, ni, 4, lambda i: harmonic(k_ref[i], k_ref[i - 1]), store_in(hx))
    wait_q()
    wait(*sent_k)
    hx[0] = harmonic(k_ref[0], hal_lon[last, 0])
    hx[ni] = harmonic(k_ref[ni - 1], hal_lon[last, 1])
    for side, j, inner in sides:
        edge_k[side] = harmonic(pack[last, side], hal_lat[last, side])
        plane[side, 0] = q_ref[:, j, :]
        plane[side, 1] = hx[pl.ds(0, ni), j, :]
        plane[side, 2] = hx[pl.ds(1, ni), j, :]
        plane[side, 3] = hy[:, max(j, inner), :]
        plane[side, 4] = hz[:, j, :]

    def radial(h, here):
        flux = h * (here - pltpu.roll(here, 1, 1))
        return pltpu.roll(flux, nr - 1, 1) - flux

    def slab(i, here, before_flux, after_flux):
        fy = hy[i] * (here - pltpu.roll(here, 1, 0))
        change = q_ref[i] + (after_flux - before_flux)
        change = change + (pltpu.roll(fy, nj - 1, 0) - fy) + radial(hz[i], here)
        return here + time_step * change

    buffers = lambda step: (t0 if step == 0 else (ta, tb)[(step - 1) % 2], (ta, tb)[step % 2])
    slot = lambda step: step + (step >= last)

    def inside(step, low, high):
        src, dst = buffers(step)

        def group(first, count):
            cells = [src[first - 1 + n] for n in range(count + 2)]
            fluxes = [hx[first + n] * (cells[n + 1] - cells[n]) for n in range(count + 1)]
            outs = [slab(first + n, cells[n + 1], fluxes[n], fluxes[n + 1]) for n in range(count)]
            for n, out in enumerate(outs):
                dst[first + n] = out

        in_groups(low, high, UNROLL, group)

    def edges(step, more):
        src, dst = buffers(step)
        for side, j, inner in sides:
            here = pack[step, side]
            before = jnp.where(plane_row == 0, hal_lon[step, 0, pl.ds(j, 1), :], pltpu.roll(here, 1, 0))
            after = jnp.where(plane_row == ni - 1, hal_lon[step, 1, pl.ds(j, 1), :], pltpu.roll(here, ni - 1, 0))
            change = plane[side, 0] + plane[side, 2] * (after - here) - plane[side, 1] * (here - before)
            change = change + plane[side, 3] * (src[:, inner, :] - here)
            change = change + edge_k[side] * (hal_lat[step, side] - here) + radial(plane[side, 4], here)
            pack[slot(step + 1), side] = here + time_step * change
        lat_copies = exchange_lat(step + 1) if more else ()
        for i, before, after in (
            (0, hal_lon[step, 0], src[1]), (ni - 1, src[ni - 2], hal_lon[step, 1])
        ):
            here = src[i]
            dst[i] = slab(i, here, hx[i] * (here - before), hx[i + 1] * (after - here))
            for side, j, _ in sides:
                dst[i, pl.ds(j, 1), :] = pack[slot(step + 1), side, pl.ds(i, 1), :]
        lon_copies = exchange_lon(step + 1, dst) if more else ()
        return lat_copies, lon_copies

    def seam(step):
        dst = buffers(step)[1]
        for side, j, _ in sides:
            dst[pl.ds(1, ni - 2), j, :] = pack[slot(step + 1), side, pl.ds(1, ni - 2), :]

    for step in range(STEPS):
        middle = 1 + UNROLL * int((ni - 2) // UNROLL * BEFORE[step])
        if step == STEPS - 1:
            middle = ni - 1
        inside(step, 1, middle)
        wait(*sent_t)
        going = edges(step, step < STEPS - 1)
        inside(step, middle, ni - 1)
        seam(step)
        wait_sent(*sent_t)
        sent_t = going
    wait_sent(*sent_k)


def stacked(x, axis):
    n = x.shape[axis]
    both = jnp.concatenate([x, x], axis=axis)
    low = both - both.astype(BF16).astype(F32)
    return jnp.where(lax.broadcasted_iota(jnp.int32, both.shape, axis) < n, both, low).astype(BF16)


def left_operand(x):
    high, low = split(jnp.concatenate([x, x], axis=1))
    col = lax.broadcasted_iota(jnp.int32, low.shape, 1)
    low = jnp.where(col < x.shape[1], low.astype(F32), 0.0).astype(BF16)
    return jnp.concatenate([high, low], axis=0)


def fold_rows(x):
    n = x.shape[0] // 2
    return x[:n] + x[n:]


def dot1(a, b, dims=NN):
    return lax.dot_general(a, b, dims, preferred_element_type=F32)


def sweep_kernel(nl, nz, t_in, k_in, q_in, u_in, v_in, w_in,
                 temp_ref, x3, lon_ref, lat_ref, rad_ref, core_ref,
                 k_ref, q_ref, u_ref, v_ref, w_ref,
                 ta, tb, hx, hy, hz, edge_k, hal_lon, hal_lat, pack, plane,
                 z1, z1t, xs, xh, f_ref, yx, small,
                 y2s, y2r, p2z, y3s, y3r, y3z, us,
                 b1s, b2s, b3s, g1s, g2s, buf, rs, zs, ag,
                 send_sem, recv_sem, halo_send, halo_recv, out_sem, in_sem):
    comm = Comm(nl, nz, send_sem, recv_sem, halo_send, halo_recv)
    t0 = tb
    ni, nj, nr = t0.shape
    t_ref = (ta, tb)[(STEPS - 1) % 2]
    r = u_ref.shape[0]
    group = 128 // r
    blocks = r // group
    per = r // nl
    wide = per * r

    fetches = {}
    for n, (source, target) in enumerate((
        (t_in, t0), (k_in, k_ref), (q_in, q_ref), (u_in, u_ref), (v_in, v_ref), (w_in, w_ref)
    )):
        fetches[n] = [pltpu.make_async_copy(source, target, in_sem.at[n, 0])]
        if n < 3:
            part = ni // 4
            fetches[n] = [
                pltpu.make_async_copy(
                    source.at[pl.ds(part * c, part)], target.at[pl.ds(part * c, part)], in_sem.at[n, c]
                )
                for c in range(4)
            ]

    def fetched(*wanted):
        for n in wanted:
            for c in fetches[n]:
                c.wait()

    barrier = pltpu.get_barrier_semaphore()
    for d in range(1, nl):
        pl.semaphore_signal(barrier, inc=1, device_id={"lon": lax.rem(comm.lon + d, nl)},
                            device_id_type=pl.DeviceIdType.MESH)
    for d in range(1, nz):
        pl.semaphore_signal(barrier, inc=1, device_id={"lat": lax.rem(comm.lat + d, nz)},
                            device_id_type=pl.DeviceIdType.MESH)
    for n in (1, 0, 2, 3, 4, 5):
        for c in fetches[n]:
            c.start()
    fetched(1, 0)

    pl.semaphore_wait(barrier, nl + nz - 2)
    conduct(comm, t0, k_ref, q_ref, ta, tb, hx, hy, hz, edge_k, hal_lon, hal_lat, pack, plane,
            lambda: fetched(2, 3, 4, 5))
    out_copy = pltpu.make_async_copy(t_ref, temp_ref, out_sem)
    out_copy.start()

    wts = split(w_ref[...])
    ut = u_ref[...]
    vt = v_ref[...]
    low_i = ni // 2
    wx = left_operand(w_ref[...])
    join = lambda x: jnp.concatenate(split(x), axis=1)

    def contract_rad(first, count):
        outs = []
        for k in range(0, count, 2):
            cells = [t_ref[first + k + e + h * low_i] for e in range(2) for h in range(2)]
            cells = jnp.concatenate([join(x) for x in cells], axis=0)
            outs.append(fold_rows(dot1(wx, cells, NT)))
        for n, out in enumerate(outs):
            z1[:, first + 2 * n, :] = out[:, : 2 * nj]
            z1[:, first + 2 * n + 1, :] = out[:, 2 * nj :]

    in_groups(0, low_i, 4, contract_rad)

    lane = lambda n, w: lax.rem(lax.broadcasted_iota(jnp.int32, (n, w), 1), 128) // r
    v4h, v4l = split(jnp.concatenate([vt.T] * group, axis=1))
    none = jnp.zeros_like(v4h)
    beside = lambda x: jnp.concatenate(
        [jnp.concatenate([x, none], axis=1), jnp.concatenate([none, x], axis=1)], axis=0
    )
    vhigh = jnp.concatenate([beside(v4h)] * 2, axis=0)
    vlow = beside(v4l)
    ux = left_operand(ut)

    def y1block(m):
        cells = jnp.concatenate([join(z1[m * group + g]) for g in range(group)], axis=0)
        both = dot1(cells, vhigh) + dot1(cells[:, : 2 * nj], vlow)
        out = both[:low_i]
        for g in range(1, group):
            out = jnp.where(lane(low_i, 256) == g, both[g * low_i : (g + 1) * low_i], out)
        out = jnp.concatenate([out[:, :128], out[:, 128:]], axis=0)
        yx[m] = join(out)
        return fold_rows(dot1(ux, stacked(out, 0)))

    if rs.shape[1] == r:
        first = comm.scatter("lon", y1block, buf, rs)
    else:
        for m in range(blocks):
            block = y1block(m)
            for c in range(r // rs.shape[1]):
                buf[m * (r // rs.shape[1]) + c] = block[c * rs.shape[1] : (c + 1) * rs.shape[1]]
        rs[comm.lon] = buf[comm.lon]
        first = comm.start("lon", lambda peer: buf.at[peer], lambda owner: rs.at[owner])

    def turn(low, high):
        for b in range(low, high):
            cell = z1[b]
            z1t[b] = stacked(jnp.concatenate([cell[:, :nj], cell[:, nj:]], axis=0).T, 1)

    turns = tuple(functools.partial(turn, r * k // 3, r * (k + 1) // 3) for k in range(3))
    finish_reduce(comm, first, rs, zs, ag, turns)

    acc = jnp.zeros((2 * r, ni), F32)
    for m in range(blocks):
        acc = acc + dot1(left_operand(ag[pl.ds(m * r, r), :]), yx[m], NT)
    acc = fold_rows(acc)
    b1s[comm.lat] = acc
    w = comm.gather("lat", b1s)
    comm.wait(w)
    b1t = total(b1s)

    bh, bl = split(jnp.concatenate([b1t] * per, axis=0).T)
    b1x = jnp.concatenate([
        jnp.concatenate([bh, bh], axis=0),
        jnp.concatenate([bl, jnp.zeros_like(bl)], axis=0),
    ], axis=1)

    def y2piece(p):
        cells = jnp.concatenate([z1t[p * per + g] for g in range(per)], axis=0)
        both = dot1(cells, b1x)
        both = both[:, :wide] + both[:, wide:]
        out = both[:nj]
        for g in range(1, per):
            out = jnp.where(lane(nj, wide) == g, both[g * nj : (g + 1) * nj], out)
        return out

    w = comm.scatter("lon", y2piece, y2s, y2r)
    g1s[comm.lon] = mmh(b1t, b1t, NT)
    g1w = comm.gather("lon", g1s)
    comm.wait(w)
    y2 = split(total(y2r))
    p2z[comm.lat] = dot3(split(vt), y2)
    w = comm.gather("lat", p2z)
    comm.wait(g1w)
    small[0] = chol_inverse(total(g1s))
    l1 = small[0]
    bd1 = split(block_diag(mmh(l1, l1, TN), per))
    lont = mmh(l1, b1t)
    lon_ref[...] = lont
    lonx = left_operand(lont)
    y2m = split(dot3(y2, bd1))

    def contract_lon(low, high):
        for j in range(low, high, 2):
            pair = jnp.concatenate(
                [stacked(t_ref[:, j, :], 0), stacked(t_ref[:, j + 1, :], 0)], axis=1
            )
            out = fold_rows(dot1(lonx, pair))
            xs[:, j, :] = out[:, :nr]
            xs[:, j + 1, :] = out[:, nr:]

    contract_lon(0, CUT)
    comm.wait(w)
    b2s[comm.lon] = dot3(split(total(p2z)), y2m, NT)
    w = comm.gather("lon", b2s)
    contract_lon(CUT, nj)
    for a in range(r):
        xh[a] = stacked(xs[a], 0)
    comm.wait(w)
    b2t = total(b2s)
    b2x = left_operand(b2t)
    parts = y3s.shape[0]
    half = per // parts

    def y3piece(h, p):
        outs = []
        first = p * per + h * half
        for g in range(0, half, 2):
            mates = [xh[first + k] for k in range(g, min(g + 2, half))]
            out = fold_rows(dot1(b2x, jnp.concatenate(mates, axis=1)))
            outs += [out[:, nr * k : nr * (k + 1)] for k in range(len(mates))]
        return jnp.concatenate(outs, axis=0)

    ws = [
        comm.scatter("lon", functools.partial(y3piece, h), y3s.at[h], y3r.at[h])
        for h in range(parts)
    ]
    g2s[comm.lat] = mmh(b2t, b2t, NT)
    g2w = comm.gather("lat", g2s)
    for h in range(parts):
        comm.wait(ws[h])
        y3z[h, comm.lat] = total(y3r.at[h])
        ws[h] = comm.gather("lat", y3z.at[h])
    comm.wait(g2w)
    small[1] = chol_inverse(total(g2s))
    l2 = small[1]
    bd2 = split(block_diag(l2, per))
    md2 = split(block_diag(mmh(l2, l2, TN), per))
    latt = mmh(l2, b2t)
    lat_ref[...] = latt
    for w in ws:
        comm.wait(w)
    whole = jnp.concatenate([total(y3z.at[h]) for h in range(parts)], axis=0)
    whole = split(whole)
    p3 = dot3(wts, whole, NT)
    y3m = dot3(md2, whole)
    b3s[comm.lon] = mm(p3, y3m)
    w = comm.gather("lon", b3s)
    y3 = split(dot3(bd2, whole))
    comm.wait(w)
    b3t = total(b3s)
    us[comm.lon] = dot3(split(b3t), y3, NT)
    w = comm.gather("lon", us)
    small[0] = chol_inverse(mmh(b3t, b3t, NT))
    l3 = small[0]
    radt = mmh(l3, b3t)
    rad_ref[...] = radt
    back_high, back_low = split(mmh(l3, radt, TN))
    back = jnp.concatenate([back_high, back_high, back_low], axis=0)
    l3h = split(l3)
    lonb = left_operand(lont.T)
    comm.wait(w)
    for p in range(nl):
        high, low = split(us[p])
        cells = jnp.concatenate([high, low, high], axis=0)
        f_ref[pl.ds(p * per, per)] = dot1(cells, back, TN).reshape(per, r, nr)
    for b in range(0, r, 2):
        pair = jnp.concatenate([stacked(f_ref[:, b + e, :], 0) for e in range(2)], axis=1)
        out = fold_rows(dot1(lonb, pair))
        x3[:, b, :] = out[:, :nr]
        x3[:, b + 1, :] = out[:, nr:]
    for p in range(nl):
        core_ref[pl.ds(p * wide, wide), :] = dot3(l3h, split(us[p])).T
    out_copy.wait()
    comm.finish()


def error_kernel(t_ref, s_ref, lon_ref, lat_ref, rad_ref, core_ref,
                 temp_out, err_out, lon_out, lat_out, rad_out, core_out, err, sem, temp_sem):
    temp_copy = pltpu.make_async_copy(t_ref, temp_out, temp_sem)
    temp_copy.start()
    latx = left_operand(lat_ref[...].T)
    ni, _, nr = t_ref.shape
    at = 16

    def chunk(c):
        part = pl.ds(c * at, at)
        return pltpu.make_async_copy(err.at[part], err_out.at[part], sem.at[c])

    @pl.loop(0, ni // at)
    def _(c):
        outs = []
        for k in range(0, at, 2):
            mates = [stacked(s_ref[c * at + k + e], 0) for e in range(2)]
            both = fold_rows(dot1(latx, jnp.concatenate(mates, axis=1)))
            outs += [both[:, :nr], both[:, nr:]]
        for k, out in enumerate(outs):
            err[c * at + k] = t_ref[c * at + k] - out
        chunk(c).start()

    lon_out[...] = lon_ref[...]
    lat_out[...] = lat_ref[...]
    rad_out[...] = rad_ref[...]
    core_out[...] = core_ref[...]

    @pl.loop(0, ni // at)
    def _(c):
        chunk(c).wait()

    temp_copy.wait()


def local(t, k, q, u, v, w):
    nl, nz = lax.axis_size("lon"), lax.axis_size("lat")
    ni, nj, nr = t.shape
    r = u.shape[1]
    rows = r * r * r // 128
    piece = rows // nl
    blocks = r * r // 128
    most = max(nl, nz)
    vm = pl.BlockSpec(memory_space=pltpu.VMEM)
    sds = lambda *s: jax.ShapeDtypeStruct(s, F32)
    V = lambda *s: pltpu.VMEM(s, F32)
    phases = 11 + 2 * PARTS
    per = r // nl
    wide = per * r
    B = lambda *s: pltpu.VMEM(s, BF16)
    parts = min(PARTS, per)
    cut = lambda n: (parts, n, wide // parts, nr)
    small = (sds(r, ni), sds(r, nj), sds(r, nr), sds(r * r, r))
    temp, s, lon, lat, rad, core = pl.pallas_call(
        functools.partial(sweep_kernel, nl, nz),
        out_shape=(sds(ni, nj, nr), sds(ni, r, nr)) + small,
        in_specs=[pl.BlockSpec(memory_space=pltpu.HBM)] * 6,
        out_specs=(pl.BlockSpec(memory_space=pl.ANY),) + (vm,) * 5,
        scratch_shapes=[
            V(ni, nj, nr), V(ni, nj, nr), V(r, ni), V(r, nj), V(r, nr),
            V(ni, nj, nr), V(ni, nj, nr), V(ni + 1, nj, nr), V(ni, nj, nr), V(ni, nj, nr),
            V(2, ni, nr), V(STEPS + 1, 2, nj, nr), V(STEPS + 1, 2, ni, nr), V(STEPS + 2, 2, ni, nr),
            V(2, 5, ni, nr), V(r, ni // 2, 2 * nj), B(r, nj, 2 * ni), V(r, nj, nr), B(r, 2 * nj, nr), V(r, r, nr),
            B(blocks, ni, 256), V(2, r, r),
            V(nl, nj, wide), V(nl, nj, wide), V(nz, r, wide),
            V(*cut(nl)), V(*cut(nl)), V(*cut(nz)), V(nl, r, wide),
            V(nz, r, ni), V(nl, r, nj), V(nl, r, nr),
            V(nl, r, r), V(nz, r, r),
            V(nl, piece, 128), V(nl, piece, 128), V(nz, piece, 128), V(rows, 128),
            pltpu.SemaphoreType.DMA((phases, most)),
            pltpu.SemaphoreType.DMA((phases, most)),
            pltpu.SemaphoreType.DMA((STEPS + 1, 4)),
            pltpu.SemaphoreType.DMA((STEPS + 1, 4)),
            pltpu.SemaphoreType.DMA,
            pltpu.SemaphoreType.DMA((6, 4)),
        ],
        compiler_params=pltpu.CompilerParams(
            collective_id=1, has_side_effects=True, vmem_limit_bytes=48 * 1024 * 1024
        ),
    )(*(pltpu.with_memory_space_constraint(x, pltpu.HBM) for x in (t, k, q, u.T, v.T, w.T)))
    anywhere = pl.BlockSpec(memory_space=pl.ANY)
    temp, err, lon, lat, rad, core = pl.pallas_call(
        error_kernel,
        out_shape=(sds(ni, nj, nr), sds(ni, nj, nr)) + small,
        in_specs=[vm] * 6,
        out_specs=(anywhere, anywhere) + (vm,) * 4,
        scratch_shapes=[
            V(ni, nj, nr), pltpu.SemaphoreType.DMA((ni // 16,)), pltpu.SemaphoreType.DMA
        ],
        compiler_params=pltpu.CompilerParams(vmem_limit_bytes=12 * 1024 * 1024),
    )(temp, s, lon, lat, rad, core)
    return temp, err, lon.T, lat.T, rad.T, core.reshape(r, r, r)


def solution(mesh):
    grid = P("lon", "lat", None)
    in_specs = (grid, grid, grid, P("lon", None), P("lat", None), P())
    out_specs = (grid, grid, P("lon", None), P("lat", None), P(), P())
    return jax.shard_map(local, mesh=mesh, in_specs=in_specs, out_specs=out_specs, check_vma=False)
```

```python
import functools

import jax
import jax.numpy as jnp
from jax import lax
from jax.experimental import pallas as pl
from jax.experimental.pallas import tpu as pltpu
from jax.sharding import PartitionSpec as P

STEPS = 4
time_step = 0.15
F32 = jnp.float32
BF16 = jnp.bfloat16
UNROLL = 6
PARTS = 2
BEFORE = (0.0, 0.3, 0.7, 1.0)
CUT = 32
NN = (((1,), (0,)), ((), ()))
NT = (((1,), (1,)), ((), ()))
TN = (((0,), (0,)), ((), ()))


def split(x):
    hi = x.astype(BF16)
    return hi, (x - hi.astype(F32)).astype(BF16)


def dot3(a, b, dims=NN):
    ah, al = a
    bh, bl = b
    d = functools.partial(lax.dot_general, dimension_numbers=dims, preferred_element_type=F32)
    return d(ah, bh) + d(ah, bl) + d(al, bh)


def mm(a, b, dims=NN):
    return dot3(split(a), split(b), dims)


def mmh(a, b, dims=NN):
    return lax.dot_general(
        a, b, dims, precision=lax.Precision.HIGHEST, preferred_element_type=F32
    )


def reciprocal(x):
    guess = pltpu.reciprocal(x, approx=True)
    return guess * (2.0 - x * guess)


def chol_inverse(gram):
    n = gram.shape[0]
    row = lax.broadcasted_iota(jnp.int32, (n, n), 0)
    col = lax.broadcasted_iota(jnp.int32, (n, n), 1)
    eye = jnp.where(row == col, 1.0, 0.0).astype(F32)
    m = jnp.concatenate([gram, eye], axis=1)
    rows = lax.broadcasted_iota(jnp.int32, m.shape, 0)
    for k in range(0, n, 2):
        first = jnp.broadcast_to(m[:, k : k + 1], m.shape)
        second = jnp.broadcast_to(m[:, k + 1 : k + 2], m.shape)
        top = m[k : k + 1, :]
        inverse = reciprocal(first[k : k + 1, :])
        ratio = first[k + 1 : k + 2, :] * inverse
        nxt = m[k + 1 : k + 2, :] - ratio * top
        if k + 2 < n:
            pivot = second[k + 1 : k + 2, :] - ratio * first[k + 1 : k + 2, :]
            update = first * inverse * top + (second - ratio * first) * reciprocal(pivot) * nxt
            m = jnp.where(rows > k + 1, m - update, jnp.where(rows == k + 1, nxt, m))
        else:
            m = jnp.where(rows == k + 1, nxt, m)
    diag = jnp.sum(jnp.where(row == col, m[:, :n], 0.0), axis=1, keepdims=True)
    return m[:, n:] / jnp.sqrt(diag)


def block_diag(x, count):
    n = x.shape[0]
    wide = jnp.concatenate([x] * count, axis=1)
    full = jnp.concatenate([wide] * count, axis=0)
    row = lax.broadcasted_iota(jnp.int32, full.shape, 0) // n
    col = lax.broadcasted_iota(jnp.int32, full.shape, 1) // n
    return jnp.where(row == col, full, 0.0)


class Comm:
    def __init__(self, nl, nz, send_sem, recv_sem, halo_send, halo_recv):
        self.halo_send, self.halo_recv = halo_send, halo_recv
        self.nl, self.nz = nl, nz
        self.lon = lax.axis_index("lon")
        self.lat = lax.axis_index("lat")
        self.send_sem, self.recv_sem = send_sem, recv_sem
        self.phase = 0
        self.sent = []

    def start(self, axis, source, target):
        count = self.nl if axis == "lon" else self.nz
        me = self.lon if axis == "lon" else self.lat
        ph = self.phase
        self.phase += 1
        waits = []
        for d in range(1, count):
            peer = lax.rem(me + d, count)
            owner = lax.rem(me + count - d, count)
            copy = pltpu.make_async_remote_copy(
                src_ref=source(peer),
                dst_ref=target(me),
                send_sem=self.send_sem.at[ph, d],
                recv_sem=self.recv_sem.at[ph, d],
                device_id={axis: peer},
                device_id_type=pl.DeviceIdType.MESH,
            )
            copy.start()
            self.sent.append(copy)
            waits.append(
                pltpu.make_async_remote_copy(
                    src_ref=target(owner),
                    dst_ref=target(owner),
                    send_sem=self.send_sem.at[ph, d],
                    recv_sem=self.recv_sem.at[ph, d],
                    device_id={axis: peer},
                    device_id_type=pl.DeviceIdType.MESH,
                )
            )
        return waits

    def scatter(self, axis, make, source, target):
        count = self.nl if axis == "lon" else self.nz
        me = self.lon if axis == "lon" else self.lat
        ph = self.phase
        self.phase += 1
        waits = []
        for d in range(1, count):
            peer = lax.rem(me + d, count)
            owner = lax.rem(me + count - d, count)
            source[peer] = make(peer)
            ends = dict(
                send_sem=self.send_sem.at[ph, d],
                recv_sem=self.recv_sem.at[ph, d],
                device_id={axis: peer},
                device_id_type=pl.DeviceIdType.MESH,
            )
            copy = pltpu.make_async_remote_copy(
                src_ref=source.at[peer], dst_ref=target.at[me], **ends
            )
            copy.start()
            self.sent.append(copy)
            waits.append(pltpu.make_async_remote_copy(
                src_ref=target.at[owner], dst_ref=target.at[owner], **ends
            ))
        target[me] = make(me)
        return waits

    def send(self, axis, shift, k, lane, source, target):
        count = self.nl if axis == "lon" else self.nz
        me = self.lon if axis == "lon" else self.lat
        return pltpu.make_async_remote_copy(
            src_ref=source,
            dst_ref=target,
            send_sem=self.halo_send.at[k, lane],
            recv_sem=self.halo_recv.at[k, lane],
            device_id={axis: lax.rem(me + shift + count, count)},
            device_id_type=pl.DeviceIdType.MESH,
        )

    def gather(self, axis, slots):
        me = self.lon if axis == "lon" else self.lat
        return self.start(axis, lambda peer: slots.at[me], lambda owner: slots.at[owner])

    def wait(self, waits):
        for w in waits:
            w.wait_recv()

    def finish(self):
        for c in self.sent:
            c.wait_send()


def total(slots):
    out = slots[0]
    for k in range(1, slots.shape[0]):
        out = out + slots[k]
    return out


def finish_reduce(comm, first, rs, zs, ag, during):
    rows = rs.shape[1]
    piece = lambda ref, p: ref.at[pl.ds(pl.multiple_of(p * rows, rows), rows)]
    during[0]()
    comm.wait(first)
    zs[comm.lat] = total(rs)
    second = comm.gather("lat", zs)
    during[1]()
    comm.wait(second)
    piece(ag, comm.lon)[...] = total(zs)
    third = comm.start("lon", lambda peer: piece(ag, comm.lon), lambda owner: piece(ag, owner))
    during[2]()
    comm.wait(third)


def harmonic(cond_a, cond_b):
    summed = cond_a + cond_b
    safe = jnp.where(summed > 0.0, summed, 1.0)
    guess = pltpu.reciprocal(safe, approx=True)
    guess = guess * (2.0 - safe * guess)
    return (cond_a + cond_a) * cond_b * guess


def in_groups(low, high, size, group):
    trips = (high - low) // size

    @pl.loop(0, trips)
    def _(trip):
        group(low + trip * size, size)

    left = max(high - low, 0) - trips * size
    if left:
        group(high - left, left)


def batched(low, high, size, values, store):
    def group(first, count):
        outs = [values(first + k) for k in range(count)]
        for k, out in enumerate(outs):
            store(first + k, out)

    in_groups(low, high, size, group)


def store_in(ref):
    def store(i, value):
        ref[i] = value

    return store


def conduct(comm, t0, k_ref, q_ref, ta, tb, hx, hy, hz, edge_k, hal_lon, hal_lat, pack, plane, wait_q):
    ni, nj, nr = t0.shape
    last = STEPS
    has_lo, has_hi = comm.lat > 0, comm.lat < comm.nz - 1
    sides = ((0, 0, 1), (1, nj - 1, nj - 2))

    def exchange_lat(k):
        copies = (
            (has_hi, has_lo, comm.send("lat", 1, k, 2, pack.at[k, 1], hal_lat.at[k, 0])),
            (has_lo, has_hi, comm.send("lat", -1, k, 3, pack.at[k, 0], hal_lat.at[k, 1])),
        )
        for out, _, c in copies:
            pl.when(out)(c.start)
        return copies

    def exchange_lon(k, src):
        copies = (
            comm.send("lon", 1, k, 0, src.at[ni - 1], hal_lon.at[k, 0]),
            comm.send("lon", -1, k, 1, src.at[0], hal_lon.at[k, 1]),
        )
        for c in copies:
            c.start()
        return copies

    def wait(lat_copies, lon_copies):
        for c in lon_copies:
            c.wait_recv()
        for _, into, c in lat_copies:
            pl.when(into)(c.wait_recv)

    def wait_sent(lat_copies, lon_copies):
        for c in lon_copies:
            c.wait_send()
        for out, _, c in lat_copies:
            pl.when(out)(c.wait_send)

    for side, j, _ in sides:
        pack[last, side] = k_ref[:, j, :]
        pack[0, side] = t0[:, j, :]
    sent_k = exchange_lat(last), exchange_lon(last, k_ref)
    sent_t = exchange_lat(0), exchange_lon(0, t0)

    @pl.when(comm.lat == 0)
    def _():
        for k in range(STEPS + 1):
            hal_lat[k, 0] = jnp.zeros((ni, nr), F32)

    @pl.when(comm.lat == comm.nz - 1)
    def _():
        for k in range(STEPS + 1):
            hal_lat[k, 1] = jnp.zeros((ni, nr), F32)

    row = lax.broadcasted_iota(jnp.int32, (nj, nr), 0)
    col = lax.broadcasted_iota(jnp.int32, (nj, nr), 1)
    plane_row = lax.broadcasted_iota(jnp.int32, (ni, nr), 0)

    def faces(i):
        k = k_ref[i]
        return (
            jnp.where(row == 0, 0.0, harmonic(k, pltpu.roll(k, 1, 0))),
            jnp.where(col == 0, 0.0, harmonic(k, pltpu.roll(k, 1, 1))),
        )

    def store_faces(i, values):
        hy[i], hz[i] = values

    batched(0, ni, 4, faces, store_faces)
    batched(1, ni, 9, lambda i: harmonic(k_ref[i], k_ref[i - 1]), store_in(hx))
    wait_q()
    wait(*sent_k)
    hx[0] = harmonic(k_ref[0], hal_lon[last, 0])
    hx[ni] = harmonic(k_ref[ni - 1], hal_lon[last, 1])
    for side, j, inner in sides:
        edge_k[side] = harmonic(pack[last, side], hal_lat[last, side])
        plane[side, 0] = q_ref[:, j, :]
        plane[side, 1] = hx[pl.ds(0, ni), j, :]
        plane[side, 2] = hx[pl.ds(1, ni), j, :]
        plane[side, 3] = hy[:, max(j, inner), :]
        plane[side, 4] = hz[:, j, :]

    def radial(h, here):
        flux = h * (here - pltpu.roll(here, 1, 1))
        return pltpu.roll(flux, nr - 1, 1) - flux

    def slab(i, here, before_flux, after_flux):
        fy = hy[i] * (here - pltpu.roll(here, 1, 0))
        change = q_ref[i] + (after_flux - before_flux)
        change = change + (pltpu.roll(fy, nj - 1, 0) - fy) + radial(hz[i], here)
        return here + time_step * change

    buffers = lambda step: (t0 if step == 0 else (ta, tb)[(step - 1) % 2], (ta, tb)[step % 2])
    slot = lambda step: step + (step >= last)

    def inside(step, low, high):
        src, dst = buffers(step)

        def group(first, count):
            cells = [src[first - 1 + n] for n in range(count + 2)]
            fluxes = [hx[first + n] * (cells[n + 1] - cells[n]) for n in range(count + 1)]
            outs = [slab(first + n, cells[n + 1], fluxes[n], fluxes[n + 1]) for n in range(count)]
            for n, out in enumerate(outs):
                dst[first + n] = out

        in_groups(low, high, UNROLL, group)

    def edges(step, more):
        src, dst = buffers(step)
        for side, j, inner in sides:
            here = pack[step, side]
            before = jnp.where(plane_row == 0, hal_lon[step, 0, pl.ds(j, 1), :], pltpu.roll(here, 1, 0))
            after = jnp.where(plane_row == ni - 1, hal_lon[step, 1, pl.ds(j, 1), :], pltpu.roll(here, ni - 1, 0))
            change = plane[side, 0] + plane[side, 2] * (after - here) - plane[side, 1] * (here - before)
            change = change + plane[side, 3] * (src[:, inner, :] - here)
            change = change + edge_k[side] * (hal_lat[step, side] - here) + radial(plane[side, 4], here)
            pack[slot(step + 1), side] = here + time_step * change
        lat_copies = exchange_lat(step + 1) if more else ()
        for i, before, after in (
            (0, hal_lon[step, 0], src[1]), (ni - 1, src[ni - 2], hal_lon[step, 1])
        ):
            here = src[i]
            dst[i] = slab(i, here, hx[i] * (here - before), hx[i + 1] * (after - here))
            for side, j, _ in sides:
                dst[i, pl.ds(j, 1), :] = pack[slot(step + 1), side, pl.ds(i, 1), :]
        lon_copies = exchange_lon(step + 1, dst) if more else ()
        return lat_copies, lon_copies

    def seam(step):
        dst = buffers(step)[1]
        for side, j, _ in sides:
            dst[pl.ds(1, ni - 2), j, :] = pack[slot(step + 1), side, pl.ds(1, ni - 2), :]

    for step in range(STEPS):
        middle = 1 + UNROLL * int((ni - 2) // UNROLL * BEFORE[step])
        if step == STEPS - 1:
            middle = ni - 1
        inside(step, 1, middle)
        wait(*sent_t)
        going = edges(step, step < STEPS - 1)
        inside(step, middle, ni - 1)
        seam(step)
        wait_sent(*sent_t)
        sent_t = going
    wait_sent(*sent_k)


def stacked(x, axis):
    n = x.shape[axis]
    both = jnp.concatenate([x, x], axis=axis)
    low = both - both.astype(BF16).astype(F32)
    return jnp.where(lax.broadcasted_iota(jnp.int32, both.shape, axis) < n, both, low).astype(BF16)


def left_operand(x):
    high, low = split(jnp.concatenate([x, x], axis=1))
    col = lax.broadcasted_iota(jnp.int32, low.shape, 1)
    low = jnp.where(col < x.shape[1], low.astype(F32), 0.0).astype(BF16)
    return jnp.concatenate([high, low], axis=0)


def fold_rows(x):
    n = x.shape[0] // 2
    return x[:n] + x[n:]


def dot1(a, b, dims=NN):
    return lax.dot_general(a, b, dims, preferred_element_type=F32)


def sweep_kernel(nl, nz, t_in, k_in, q_in, u_in, v_in, w_in,
                 temp_ref, x3, lon_ref, lat_ref, rad_ref, core_ref,
                 k_ref, q_ref, u_ref, v_ref, w_ref,
                 ta, tb, hx, hy, hz, edge_k, hal_lon, hal_lat, pack, plane,
                 z1, z1t, xs, xh, f_ref, yx, small,
                 y2s, y2r, p2z, y3s, y3r, y3z, us,
                 b1s, b2s, b3s, g1s, g2s, buf, rs, zs, ag,
                 send_sem, recv_sem, halo_send, halo_recv, out_sem, in_sem):
    comm = Comm(nl, nz, send_sem, recv_sem, halo_send, halo_recv)
    t0 = tb
    ni, nj, nr = t0.shape
    t_ref = (ta, tb)[(STEPS - 1) % 2]
    r = u_ref.shape[0]
    group = 128 // r
    blocks = r // group
    per = r // nl
    wide = per * r

    fetches = {}
    for n, (source, target) in enumerate((
        (t_in, t0), (k_in, k_ref), (q_in, q_ref), (u_in, u_ref), (v_in, v_ref), (w_in, w_ref)
    )):
        fetches[n] = [pltpu.make_async_copy(source, target, in_sem.at[n, 0])]
        if n < 3:
            part = ni // 4
            fetches[n] = [
                pltpu.make_async_copy(
                    source.at[pl.ds(part * c, part)], target.at[pl.ds(part * c, part)], in_sem.at[n, c]
                )
                for c in range(4)
            ]

    def fetched(*wanted):
        for n in wanted:
            for c in fetches[n]:
                c.wait()

    barrier = pltpu.get_barrier_semaphore()
    for d in range(1, nl):
        pl.semaphore_signal(barrier, inc=1, device_id={"lon": lax.rem(comm.lon + d, nl)},
                            device_id_type=pl.DeviceIdType.MESH)
    for d in range(1, nz):
        pl.semaphore_signal(barrier, inc=1, device_id={"lat": lax.rem(comm.lat + d, nz)},
                            device_id_type=pl.DeviceIdType.MESH)
    for n in (1, 0, 2, 3, 4, 5):
        for c in fetches[n]:
            c.start()
    fetched(1, 0)

    pl.semaphore_wait(barrier, nl + nz - 2)
    conduct(comm, t0, k_ref, q_ref, ta, tb, hx, hy, hz, edge_k, hal_lon, hal_lat, pack, plane,
            lambda: fetched(2, 3, 4, 5))
    out_copy = pltpu.make_async_copy(t_ref, temp_ref, out_sem)
    out_copy.start()

    wts = split(w_ref[...])
    ut = u_ref[...]
    vt = v_ref[...]
    low_i = ni // 2
    wx = left_operand(w_ref[...])
    join = lambda x: jnp.concatenate(split(x), axis=1)

    def contract_rad(first, count):
        outs = []
        for k in range(0, count, 2):
            cells = [t_ref[first + k + e + h * low_i] for e in range(2) for h in range(2)]
            cells = jnp.concatenate([join(x) for x in cells], axis=0)
            outs.append(fold_rows(dot1(wx, cells, NT)))
        for n, out in enumerate(outs):
            z1[:, first + 2 * n, :] = out[:, : 2 * nj]
            z1[:, first + 2 * n + 1, :] = out[:, 2 * nj :]

    in_groups(0, low_i, 8, contract_rad)

    lane = lambda n, w: lax.rem(lax.broadcasted_iota(jnp.int32, (n, w), 1), 128) // r
    v4h, v4l = split(jnp.concatenate([vt.T] * group, axis=1))
    none = jnp.zeros_like(v4h)
    beside = lambda x: jnp.concatenate(
        [jnp.concatenate([x, none], axis=1), jnp.concatenate([none, x], axis=1)], axis=0
    )
    vhigh = jnp.concatenate([beside(v4h)] * 2, axis=0)
    vlow = beside(v4l)
    ux = left_operand(ut)

    def y1block(m):
        cells = jnp.concatenate([join(z1[m * group + g]) for g in range(group)], axis=0)
        both = dot1(cells, vhigh) + dot1(cells[:, : 2 * nj], vlow)
        out = both[:low_i]
        for g in range(1, group):
            out = jnp.where(lane(low_i, 256) == g, both[g * low_i : (g + 1) * low_i], out)
        out = jnp.concatenate([out[:, :128], out[:, 128:]], axis=0)
        yx[m] = join(out)
        return fold_rows(dot1(ux, stacked(out, 0)))

    if rs.shape[1] == r:
        first = comm.scatter("lon", y1block, buf, rs)
    else:
        for m in range(blocks):
            block = y1block(m)
            for c in range(r // rs.shape[1]):
                buf[m * (r // rs.shape[1]) + c] = block[c * rs.shape[1] : (c + 1) * rs.shape[1]]
        rs[comm.lon] = buf[comm.lon]
        first = comm.start("lon", lambda peer: buf.at[peer], lambda owner: rs.at[owner])

    def turn(low, high):
        for b in range(low, high):
            cell = z1[b]
            z1t[b] = stacked(jnp.concatenate([cell[:, :nj], cell[:, nj:]], axis=0).T, 1)

    turns = tuple(functools.partial(turn, r * k // 3, r * (k + 1) // 3) for k in range(3))
    finish_reduce(comm, first, rs, zs, ag, turns)

    acc = jnp.zeros((2 * r, ni), F32)
    for m in range(blocks):
        acc = acc + dot1(left_operand(ag[pl.ds(m * r, r), :]), yx[m], NT)
    acc = fold_rows(acc)
    b1s[comm.lat] = acc
    w = comm.gather("lat", b1s)
    comm.wait(w)
    b1t = total(b1s)

    bh, bl = split(jnp.concatenate([b1t] * per, axis=0).T)
    b1x = jnp.concatenate([
        jnp.concatenate([bh, bh], axis=0),
        jnp.concatenate([bl, jnp.zeros_like(bl)], axis=0),
    ], axis=1)

    def y2piece(p):
        cells = jnp.concatenate([z1t[p * per + g] for g in range(per)], axis=0)
        both = dot1(cells, b1x)
        both = both[:, :wide] + both[:, wide:]
        out = both[:nj]
        for g in range(1, per):
            out = jnp.where(lane(nj, wide) == g, both[g * nj : (g + 1) * nj], out)
        return out

    w = comm.scatter("lon", y2piece, y2s, y2r)
    g1s[comm.lon] = mmh(b1t, b1t, NT)
    g1w = comm.gather("lon", g1s)
    comm.wait(w)
    y2 = split(total(y2r))
    p2z[comm.lat] = dot3(split(vt), y2)
    w = comm.gather("lat", p2z)
    comm.wait(g1w)
    small[0] = chol_inverse(total(g1s))
    l1 = small[0]
    bd1 = split(block_diag(mmh(l1, l1, TN), per))
    lont = mmh(l1, b1t)
    lon_ref[...] = lont
    lonx = left_operand(lont)
    y2m = split(dot3(y2, bd1))

    def contract_lon(low, high):
        for j in range(low, high, 2):
            pair = jnp.concatenate(
                [stacked(t_ref[:, j, :], 0), stacked(t_ref[:, j + 1, :], 0)], axis=1
            )
            out = fold_rows(dot1(lonx, pair))
            xs[:, j, :] = out[:, :nr]
            xs[:, j + 1, :] = out[:, nr:]

    contract_lon(0, CUT)
    comm.wait(w)
    b2s[comm.lon] = dot3(split(total(p2z)), y2m, NT)
    w = comm.gather("lon", b2s)
    contract_lon(CUT, nj)
    for a in range(r):
        xh[a] = stacked(xs[a], 0)
    comm.wait(w)
    b2t = total(b2s)
    b2x = left_operand(b2t)
    parts = y3s.shape[0]
    half = per // parts

    def y3piece(h, p):
        outs = []
        first = p * per + h * half
        for g in range(0, half, 2):
            mates = [xh[first + k] for k in range(g, min(g + 2, half))]
            out = fold_rows(dot1(b2x, jnp.concatenate(mates, axis=1)))
            outs += [out[:, nr * k : nr * (k + 1)] for k in range(len(mates))]
        return jnp.concatenate(outs, axis=0)

    ws = [
        comm.scatter("lon", functools.partial(y3piece, h), y3s.at[h], y3r.at[h])
        for h in range(parts)
    ]
    g2s[comm.lat] = mmh(b2t, b2t, NT)
    g2w = comm.gather("lat", g2s)
    for h in range(parts):
        comm.wait(ws[h])
        y3z[h, comm.lat] = total(y3r.at[h])
        ws[h] = comm.gather("lat", y3z.at[h])
    comm.wait(g2w)
    small[1] = chol_inverse(total(g2s))
    l2 = small[1]
    bd2 = split(block_diag(l2, per))
    md2 = split(block_diag(mmh(l2, l2, TN), per))
    latt = mmh(l2, b2t)
    lat_ref[...] = latt
    for w in ws:
        comm.wait(w)
    whole = jnp.concatenate([total(y3z.at[h]) for h in range(parts)], axis=0)
    whole = split(whole)
    p3 = dot3(wts, whole, NT)
    y3m = dot3(md2, whole)
    b3s[comm.lon] = mm(p3, y3m)
    w = comm.gather("lon", b3s)
    y3 = split(dot3(bd2, whole))
    comm.wait(w)
    b3t = total(b3s)
    us[comm.lon] = dot3(split(b3t), y3, NT)
    w = comm.gather("lon", us)
    small[0] = chol_inverse(mmh(b3t, b3t, NT))
    l3 = small[0]
    radt = mmh(l3, b3t)
    rad_ref[...] = radt
    back_high, back_low = split(mmh(l3, radt, TN))
    back = jnp.concatenate([back_high, back_high, back_low], axis=0)
    l3h = split(l3)
    lonb = left_operand(lont.T)
    comm.wait(w)
    for p in range(nl):
        high, low = split(us[p])
        cells = jnp.concatenate([high, low, high], axis=0)
        f_ref[pl.ds(p * per, per)] = dot1(cells, back, TN).reshape(per, r, nr)
    for b in range(0, r, 2):
        pair = jnp.concatenate([stacked(f_ref[:, b + e, :], 0) for e in range(2)], axis=1)
        out = fold_rows(dot1(lonb, pair))
        x3[:, b, :] = out[:, :nr]
        x3[:, b + 1, :] = out[:, nr:]
    for p in range(nl):
        core_ref[pl.ds(p * wide, wide), :] = dot3(l3h, split(us[p])).T
    out_copy.wait()
    comm.finish()


def error_kernel(t_ref, s_ref, lon_ref, lat_ref, rad_ref, core_ref,
                 temp_out, err_out, lon_out, lat_out, rad_out, core_out, err, sem, temp_sem):
    temp_copy = pltpu.make_async_copy(t_ref, temp_out, temp_sem)
    temp_copy.start()
    latx = left_operand(lat_ref[...].T)
    ni, _, nr = t_ref.shape
    at = 32

    def chunk(c):
        part = pl.ds(c * at, at)
        return pltpu.make_async_copy(err.at[part], err_out.at[part], sem.at[c])

    @pl.loop(0, ni // at)
    def _(c):
        outs = []
        for k in range(0, at, 2):
            mates = [stacked(s_ref[c * at + k + e], 0) for e in range(2)]
            both = fold_rows(dot1(latx, jnp.concatenate(mates, axis=1)))
            outs += [both[:, :nr], both[:, nr:]]
        for k, out in enumerate(outs):
            err[c * at + k] = t_ref[c * at + k] - out
        chunk(c).start()

    lon_out[...] = lon_ref[...]
    lat_out[...] = lat_ref[...]
    rad_out[...] = rad_ref[...]
    core_out[...] = core_ref[...]

    @pl.loop(0, ni // at)
    def _(c):
        chunk(c).wait()

    temp_copy.wait()


def local(t, k, q, u, v, w):
    nl, nz = lax.axis_size("lon"), lax.axis_size("lat")
    ni, nj, nr = t.shape
    r = u.shape[1]
    rows = r * r * r // 128
    piece = rows // nl
    blocks = r * r // 128
    most = max(nl, nz)
    vm = pl.BlockSpec(memory_space=pltpu.VMEM)
    sds = lambda *s: jax.ShapeDtypeStruct(s, F32)
    V = lambda *s: pltpu.VMEM(s, F32)
    phases = 11 + 2 * PARTS
    per = r // nl
    wide = per * r
    B = lambda *s: pltpu.VMEM(s, BF16)
    parts = min(PARTS, per)
    cut = lambda n: (parts, n, wide // parts, nr)
    small = (sds(r, ni), sds(r, nj), sds(r, nr), sds(r * r, r))
    temp, s, lon, lat, rad, core = pl.pallas_call(
        functools.partial(sweep_kernel, nl, nz),
        out_shape=(sds(ni, nj, nr), sds(ni, r, nr)) + small,
        in_specs=[pl.BlockSpec(memory_space=pltpu.HBM)] * 6,
        out_specs=(pl.BlockSpec(memory_space=pl.ANY),) + (vm,) * 5,
        scratch_shapes=[
            V(ni, nj, nr), V(ni, nj, nr), V(r, ni), V(r, nj), V(r, nr),
            V(ni, nj, nr), V(ni, nj, nr), V(ni + 1, nj, nr), V(ni, nj, nr), V(ni, nj, nr),
            V(2, ni, nr), V(STEPS + 1, 2, nj, nr), V(STEPS + 1, 2, ni, nr), V(STEPS + 2, 2, ni, nr),
            V(2, 5, ni, nr), V(r, ni // 2, 2 * nj), B(r, nj, 2 * ni), V(r, nj, nr), B(r, 2 * nj, nr), V(r, r, nr),
            B(blocks, ni, 256), V(2, r, r),
            V(nl, nj, wide), V(nl, nj, wide), V(nz, r, wide),
            V(*cut(nl)), V(*cut(nl)), V(*cut(nz)), V(nl, r, wide),
            V(nz, r, ni), V(nl, r, nj), V(nl, r, nr),
            V(nl, r, r), V(nz, r, r),
            V(nl, piece, 128), V(nl, piece, 128), V(nz, piece, 128), V(rows, 128),
            pltpu.SemaphoreType.DMA((phases, most)),
            pltpu.SemaphoreType.DMA((phases, most)),
            pltpu.SemaphoreType.DMA((STEPS + 1, 4)),
            pltpu.SemaphoreType.DMA((STEPS + 1, 4)),
            pltpu.SemaphoreType.DMA,
            pltpu.SemaphoreType.DMA((6, 4)),
        ],
        compiler_params=pltpu.CompilerParams(
            collective_id=1, has_side_effects=True, vmem_limit_bytes=48 * 1024 * 1024
        ),
    )(*(pltpu.with_memory_space_constraint(x, pltpu.HBM) for x in (t, k, q, u.T, v.T, w.T)))
    anywhere = pl.BlockSpec(memory_space=pl.ANY)
    temp, err, lon, lat, rad, core = pl.pallas_call(
        error_kernel,
        out_shape=(sds(ni, nj, nr), sds(ni, nj, nr)) + small,
        in_specs=[vm] * 6,
        out_specs=(anywhere, anywhere) + (vm,) * 4,
        scratch_shapes=[
            V(ni, nj, nr), pltpu.SemaphoreType.DMA((ni // 32,)), pltpu.SemaphoreType.DMA
        ],
        compiler_params=pltpu.CompilerParams(vmem_limit_bytes=12 * 1024 * 1024),
    )(temp, s, lon, lat, rad, core)
    return temp, err, lon.T, lat.T, rad.T, core.reshape(r, r, r)


def solution(mesh):
    grid = P("lon", "lat", None)
    in_specs = (grid, grid, grid, P("lon", None), P("lat", None), P())
    out_specs = (grid, grid, P("lon", None), P("lat", None), P(), P())
    return jax.shard_map(local, mesh=mesh, in_specs=in_specs, out_specs=out_specs, check_vma=False)
```

```python
import functools

import jax
import jax.numpy as jnp
from jax import lax
from jax.experimental import pallas as pl
from jax.experimental.pallas import tpu as pltpu
from jax.sharding import PartitionSpec as P

STEPS = 4
time_step = 0.15
F32 = jnp.float32
BF16 = jnp.bfloat16
UNROLL = 6
PARTS = 2
BEFORE = (0.0, 0.3, 0.7, 1.0)
CUT = 32
NN = (((1,), (0,)), ((), ()))
NT = (((1,), (1,)), ((), ()))
TN = (((0,), (0,)), ((), ()))


def split(x):
    hi = x.astype(BF16)
    return hi, (x - hi.astype(F32)).astype(BF16)


def dot3(a, b, dims=NN):
    ah, al = a
    bh, bl = b
    d = functools.partial(lax.dot_general, dimension_numbers=dims, preferred_element_type=F32)
    return d(ah, bh) + d(ah, bl) + d(al, bh)


def mm(a, b, dims=NN):
    return dot3(split(a), split(b), dims)


def mmh(a, b, dims=NN):
    return lax.dot_general(
        a, b, dims, precision=lax.Precision.HIGHEST, preferred_element_type=F32
    )


def reciprocal(x):
    guess = pltpu.reciprocal(x, approx=True)
    return guess * (2.0 - x * guess)


def chol_inverse(gram):
    n = gram.shape[0]
    row = lax.broadcasted_iota(jnp.int32, (n, n), 0)
    col = lax.broadcasted_iota(jnp.int32, (n, n), 1)
    eye = jnp.where(row == col, 1.0, 0.0).astype(F32)
    m = jnp.concatenate([gram, eye], axis=1)
    rows = lax.broadcasted_iota(jnp.int32, m.shape, 0)
    for k in range(0, n, 2):
        first = jnp.broadcast_to(m[:, k : k + 1], m.shape)
        second = jnp.broadcast_to(m[:, k + 1 : k + 2], m.shape)
        top = m[k : k + 1, :]
        inverse = reciprocal(first[k : k + 1, :])
        ratio = first[k + 1 : k + 2, :] * inverse
        nxt = m[k + 1 : k + 2, :] - ratio * top
        if k + 2 < n:
            pivot = second[k + 1 : k + 2, :] - ratio * first[k + 1 : k + 2, :]
            update = first * inverse * top + (second - ratio * first) * reciprocal(pivot) * nxt
            m = jnp.where(rows > k + 1, m - update, jnp.where(rows == k + 1, nxt, m))
        else:
            m = jnp.where(rows == k + 1, nxt, m)
    diag = jnp.sum(jnp.where(row == col, m[:, :n], 0.0), axis=1, keepdims=True)
    return m[:, n:] / jnp.sqrt(diag)


def block_diag(x, count):
    n = x.shape[0]
    wide = jnp.concatenate([x] * count, axis=1)
    full = jnp.concatenate([wide] * count, axis=0)
    row = lax.broadcasted_iota(jnp.int32, full.shape, 0) // n
    col = lax.broadcasted_iota(jnp.int32, full.shape, 1) // n
    return jnp.where(row == col, full, 0.0)


class Comm:
    def __init__(self, nl, nz, send_sem, recv_sem, halo_send, halo_recv):
        self.halo_send, self.halo_recv = halo_send, halo_recv
        self.nl, self.nz = nl, nz
        self.lon = lax.axis_index("lon")
        self.lat = lax.axis_index("lat")
        self.send_sem, self.recv_sem = send_sem, recv_sem
        self.phase = 0
        self.sent = []

    def start(self, axis, source, target):
        count = self.nl if axis == "lon" else self.nz
        me = self.lon if axis == "lon" else self.lat
        ph = self.phase
        self.phase += 1
        waits = []
        for d in range(1, count):
            peer = lax.rem(me + d, count)
            owner = lax.rem(me + count - d, count)
            copy = pltpu.make_async_remote_copy(
                src_ref=source(peer),
                dst_ref=target(me),
                send_sem=self.send_sem.at[ph, d],
                recv_sem=self.recv_sem.at[ph, d],
                device_id={axis: peer},
                device_id_type=pl.DeviceIdType.MESH,
            )
            copy.start()
            self.sent.append(copy)
            waits.append(
                pltpu.make_async_remote_copy(
                    src_ref=target(owner),
                    dst_ref=target(owner),
                    send_sem=self.send_sem.at[ph, d],
                    recv_sem=self.recv_sem.at[ph, d],
                    device_id={axis: peer},
                    device_id_type=pl.DeviceIdType.MESH,
                )
            )
        return waits

    def scatter(self, axis, make, source, target):
        count = self.nl if axis == "lon" else self.nz
        me = self.lon if axis == "lon" else self.lat
        ph = self.phase
        self.phase += 1
        waits = []
        for d in range(1, count):
            peer = lax.rem(me + d, count)
            owner = lax.rem(me + count - d, count)
            source[peer] = make(peer)
            ends = dict(
                send_sem=self.send_sem.at[ph, d],
                recv_sem=self.recv_sem.at[ph, d],
                device_id={axis: peer},
                device_id_type=pl.DeviceIdType.MESH,
            )
            copy = pltpu.make_async_remote_copy(
                src_ref=source.at[peer], dst_ref=target.at[me], **ends
            )
            copy.start()
            self.sent.append(copy)
            waits.append(pltpu.make_async_remote_copy(
                src_ref=target.at[owner], dst_ref=target.at[owner], **ends
            ))
        target[me] = make(me)
        return waits

    def send(self, axis, shift, k, lane, source, target):
        count = self.nl if axis == "lon" else self.nz
        me = self.lon if axis == "lon" else self.lat
        return pltpu.make_async_remote_copy(
            src_ref=source,
            dst_ref=target,
            send_sem=self.halo_send.at[k, lane],
            recv_sem=self.halo_recv.at[k, lane],
            device_id={axis: lax.rem(me + shift + count, count)},
            device_id_type=pl.DeviceIdType.MESH,
        )

    def gather(self, axis, slots):
        me = self.lon if axis == "lon" else self.lat
        return self.start(axis, lambda peer: slots.at[me], lambda owner: slots.at[owner])

    def wait(self, waits):
        for w in waits:
            w.wait_recv()

    def finish(self):
        for c in self.sent:
            c.wait_send()


def total(slots):
    out = slots[0]
    for k in range(1, slots.shape[0]):
        out = out + slots[k]
    return out


def finish_reduce(comm, first, rs, zs, ag, during):
    rows = rs.shape[1]
    piece = lambda ref, p: ref.at[pl.ds(pl.multiple_of(p * rows, rows), rows)]
    during[0]()
    comm.wait(first)
    zs[comm.lat] = total(rs)
    second = comm.gather("lat", zs)
    during[1]()
    comm.wait(second)
    piece(ag, comm.lon)[...] = total(zs)
    third = comm.start("lon", lambda peer: piece(ag, comm.lon), lambda owner: piece(ag, owner))
    during[2]()
    comm.wait(third)


def harmonic(cond_a, cond_b):
    summed = cond_a + cond_b
    safe = jnp.where(summed > 0.0, summed, 1.0)
    guess = pltpu.reciprocal(safe, approx=True)
    guess = guess * (2.0 - safe * guess)
    return (cond_a + cond_a) * cond_b * guess


def in_groups(low, high, size, group):
    trips = (high - low) // size

    @pl.loop(0, trips)
    def _(trip):
        group(low + trip * size, size)

    left = max(high - low, 0) - trips * size
    if left:
        group(high - left, left)


def batched(low, high, size, values, store):
    def group(first, count):
        outs = [values(first + k) for k in range(count)]
        for k, out in enumerate(outs):
            store(first + k, out)

    in_groups(low, high, size, group)


def store_in(ref):
    def store(i, value):
        ref[i] = value

    return store


def conduct(comm, t0, k_ref, q_ref, ta, tb, hx, hy, hz, edge_k, hal_lon, hal_lat, pack, plane, wait_q):
    ni, nj, nr = t0.shape
    last = STEPS
    has_lo, has_hi = comm.lat > 0, comm.lat < comm.nz - 1
    sides = ((0, 0, 1), (1, nj - 1, nj - 2))

    def exchange_lat(k):
        copies = (
            (has_hi, has_lo, comm.send("lat", 1, k, 2, pack.at[k, 1], hal_lat.at[k, 0])),
            (has_lo, has_hi, comm.send("lat", -1, k, 3, pack.at[k, 0], hal_lat.at[k, 1])),
        )
        for out, _, c in copies:
            pl.when(out)(c.start)
        return copies

    def exchange_lon(k, src):
        copies = (
            comm.send("lon", 1, k, 0, src.at[ni - 1], hal_lon.at[k, 0]),
            comm.send("lon", -1, k, 1, src.at[0], hal_lon.at[k, 1]),
        )
        for c in copies:
            c.start()
        return copies

    def wait(lat_copies, lon_copies):
        for c in lon_copies:
            c.wait_recv()
        for _, into, c in lat_copies:
            pl.when(into)(c.wait_recv)

    def wait_sent(lat_copies, lon_copies):
        for c in lon_copies:
            c.wait_send()
        for out, _, c in lat_copies:
            pl.when(out)(c.wait_send)

    for side, j, _ in sides:
        pack[last, side] = k_ref[:, j, :]
        pack[0, side] = t0[:, j, :]
    sent_k = exchange_lat(last), exchange_lon(last, k_ref)
    sent_t = exchange_lat(0), exchange_lon(0, t0)

    @pl.when(comm.lat == 0)
    def _():
        for k in range(STEPS + 1):
            hal_lat[k, 0] = jnp.zeros((ni, nr), F32)

    @pl.when(comm.lat == comm.nz - 1)
    def _():
        for k in range(STEPS + 1):
            hal_lat[k, 1] = jnp.zeros((ni, nr), F32)

    row = lax.broadcasted_iota(jnp.int32, (nj, nr), 0)
    col = lax.broadcasted_iota(jnp.int32, (nj, nr), 1)
    plane_row = lax.broadcasted_iota(jnp.int32, (ni, nr), 0)

    def faces(i):
        k = k_ref[i]
        return (
            jnp.where(row == 0, 0.0, harmonic(k, pltpu.roll(k, 1, 0))),
            jnp.where(col == 0, 0.0, harmonic(k, pltpu.roll(k, 1, 1))),
        )

    def store_faces(i, values):
        hy[i], hz[i] = values

    batched(0, ni, 4, faces, store_faces)
    batched(1, ni, 9, lambda i: harmonic(k_ref[i], k_ref[i - 1]), store_in(hx))
    wait_q()
    wait(*sent_k)
    hx[0] = harmonic(k_ref[0], hal_lon[last, 0])
    hx[ni] = harmonic(k_ref[ni - 1], hal_lon[last, 1])
    for side, j, inner in sides:
        edge_k[side] = harmonic(pack[last, side], hal_lat[last, side])
        plane[side, 0] = q_ref[:, j, :]
        plane[side, 1] = hx[pl.ds(0, ni), j, :]
        plane[side, 2] = hx[pl.ds(1, ni), j, :]
        plane[side, 3] = hy[:, max(j, inner), :]
        plane[side, 4] = hz[:, j, :]

    def radial(h, here):
        flux = h * (here - pltpu.roll(here, 1, 1))
        return pltpu.roll(flux, nr - 1, 1) - flux

    def slab(i, here, before_flux, after_flux):
        fy = hy[i] * (here - pltpu.roll(here, 1, 0))
        change = q_ref[i] + (after_flux - before_flux)
        change = change + (pltpu.roll(fy, nj - 1, 0) - fy) + radial(hz[i], here)
        return here + time_step * change

    buffers = lambda step: (t0 if step == 0 else (ta, tb)[(step - 1) % 2], (ta, tb)[step % 2])
    slot = lambda step: step + (step >= last)

    def inside(step, low, high):
        src, dst = buffers(step)

        def group(first, count):
            cells = [src[first - 1 + n] for n in range(count + 2)]
            fluxes = [hx[first + n] * (cells[n + 1] - cells[n]) for n in range(count + 1)]
            outs = [slab(first + n, cells[n + 1], fluxes[n], fluxes[n + 1]) for n in range(count)]
            for n, out in enumerate(outs):
                dst[first + n] = out

        in_groups(low, high, UNROLL, group)

    def edges(step, more):
        src, dst = buffers(step)
        for side, j, inner in sides:
            here = pack[step, side]
            before = jnp.where(plane_row == 0, hal_lon[step, 0, pl.ds(j, 1), :], pltpu.roll(here, 1, 0))
            after = jnp.where(plane_row == ni - 1, hal_lon[step, 1, pl.ds(j, 1), :], pltpu.roll(here, ni - 1, 0))
            change = plane[side, 0] + plane[side, 2] * (after - here) - plane[side, 1] * (here - before)
            change = change + plane[side, 3] * (src[:, inner, :] - here)
            change = change + edge_k[side] * (hal_lat[step, side] - here) + radial(plane[side, 4], here)
            pack[slot(step + 1), side] = here + time_step * change
        lat_copies = exchange_lat(step + 1) if more else ()
        for i, before, after in (
            (0, hal_lon[step, 0], src[1]), (ni - 1, src[ni - 2], hal_lon[step, 1])
        ):
            here = src[i]
            dst[i] = slab(i, here, hx[i] * (here - before), hx[i + 1] * (after - here))
            for side, j, _ in sides:
                dst[i, pl.ds(j, 1), :] = pack[slot(step + 1), side, pl.ds(i, 1), :]
        lon_copies = exchange_lon(step + 1, dst) if more else ()
        return lat_copies, lon_copies

    def seam(step):
        dst = buffers(step)[1]
        for side, j, _ in sides:
            dst[pl.ds(1, ni - 2), j, :] = pack[slot(step + 1), side, pl.ds(1, ni - 2), :]

    for step in range(STEPS):
        middle = 1 + UNROLL * int((ni - 2) // UNROLL * BEFORE[step])
        if step == STEPS - 1:
            middle = ni - 1
        inside(step, 1, middle)
        wait(*sent_t)
        going = edges(step, step < STEPS - 1)
        inside(step, middle, ni - 1)
        seam(step)
        wait_sent(*sent_t)
        sent_t = going
    wait_sent(*sent_k)


def stacked(x, axis):
    n = x.shape[axis]
    both = jnp.concatenate([x, x], axis=axis)
    low = both - both.astype(BF16).astype(F32)
    return jnp.where(lax.broadcasted_iota(jnp.int32, both.shape, axis) < n, both, low).astype(BF16)


def left_operand(x):
    high, low = split(jnp.concatenate([x, x], axis=1))
    col = lax.broadcasted_iota(jnp.int32, low.shape, 1)
    low = jnp.where(col < x.shape[1], low.astype(F32), 0.0).astype(BF16)
    return jnp.concatenate([high, low], axis=0)


def fold_rows(x):
    n = x.shape[0] // 2
    return x[:n] + x[n:]


def dot1(a, b, dims=NN):
    return lax.dot_general(a, b, dims, preferred_element_type=F32)


def sweep_kernel(nl, nz, t_in, k_in, q_in, u_in, v_in, w_in,
                 temp_ref, x3, lon_ref, lat_ref, rad_ref, core_ref,
                 k_ref, q_ref, u_ref, v_ref, w_ref,
                 ta, tb, hx, hy, hz, edge_k, hal_lon, hal_lat, pack, plane,
                 z1, z1t, xs, xh, f_ref, yx, small,
                 y2s, y2r, p2z, y3s, y3r, y3z, us,
                 b1s, b2s, b3s, g1s, g2s, buf, rs, zs, ag,
                 send_sem, recv_sem, halo_send, halo_recv, out_sem, in_sem):
    comm = Comm(nl, nz, send_sem, recv_sem, halo_send, halo_recv)
    t0 = tb
    ni, nj, nr = t0.shape
    t_ref = (ta, tb)[(STEPS - 1) % 2]
    r = u_ref.shape[0]
    group = 128 // r
    blocks = r // group
    per = r // nl
    wide = per * r

    fetches = {}
    for n, (source, target) in enumerate((
        (t_in, t0), (k_in, k_ref), (q_in, q_ref), (u_in, u_ref), (v_in, v_ref), (w_in, w_ref)
    )):
        fetches[n] = [pltpu.make_async_copy(source, target, in_sem.at[n, 0])]
        if n < 3:
            part = ni // 4
            fetches[n] = [
                pltpu.make_async_copy(
                    source.at[pl.ds(part * c, part)], target.at[pl.ds(part * c, part)], in_sem.at[n, c]
                )
                for c in range(4)
            ]

    def fetched(*wanted):
        for n in wanted:
            for c in fetches[n]:
                c.wait()

    barrier = pltpu.get_barrier_semaphore()
    for d in range(1, nl):
        pl.semaphore_signal(barrier, inc=1, device_id={"lon": lax.rem(comm.lon + d, nl)},
                            device_id_type=pl.DeviceIdType.MESH)
    for d in range(1, nz):
        pl.semaphore_signal(barrier, inc=1, device_id={"lat": lax.rem(comm.lat + d, nz)},
                            device_id_type=pl.DeviceIdType.MESH)
    for n in (1, 0, 2, 3, 4, 5):
        for c in fetches[n]:
            c.start()
    fetched(1, 0)

    pl.semaphore_wait(barrier, nl + nz - 2)
    conduct(comm, t0, k_ref, q_ref, ta, tb, hx, hy, hz, edge_k, hal_lon, hal_lat, pack, plane,
            lambda: fetched(2, 3, 4, 5))
    out_copy = pltpu.make_async_copy(t_ref, temp_ref, out_sem)
    out_copy.start()

    wts = split(w_ref[...])
    ut = u_ref[...]
    vt = v_ref[...]
    low_i = ni // 2
    wx = left_operand(w_ref[...])
    join = lambda x: jnp.concatenate(split(x), axis=1)

    def contract_rad(first, count):
        outs = []
        for k in range(0, count, 2):
            cells = [t_ref[first + k + e + h * low_i] for e in range(2) for h in range(2)]
            cells = jnp.concatenate([join(x) for x in cells], axis=0)
            outs.append(fold_rows(dot1(wx, cells, NT)))
        for n, out in enumerate(outs):
            z1[:, first + 2 * n, :] = out[:, : 2 * nj]
            z1[:, first + 2 * n + 1, :] = out[:, 2 * nj :]

    in_groups(0, low_i, 8, contract_rad)

    lane = lambda n, w: lax.rem(lax.broadcasted_iota(jnp.int32, (n, w), 1), 128) // r
    v4h, v4l = split(jnp.concatenate([vt.T] * group, axis=1))
    none = jnp.zeros_like(v4h)
    beside = lambda x: jnp.concatenate(
        [jnp.concatenate([x, none], axis=1), jnp.concatenate([none, x], axis=1)], axis=0
    )
    vhigh = jnp.concatenate([beside(v4h)] * 2, axis=0)
    vlow = beside(v4l)
    ux = left_operand(ut)

    def y1block(m):
        cells = jnp.concatenate([join(z1[m * group + g]) for g in range(group)], axis=0)
        both = dot1(cells, vhigh) + dot1(cells[:, : 2 * nj], vlow)
        out = both[:low_i]
        for g in range(1, group):
            out = jnp.where(lane(low_i, 256) == g, both[g * low_i : (g + 1) * low_i], out)
        out = jnp.concatenate([out[:, :128], out[:, 128:]], axis=0)
        yx[m] = join(out)
        return fold_rows(dot1(ux, stacked(out, 0)))

    if rs.shape[1] == r:
        first = comm.scatter("lon", y1block, buf, rs)
    else:
        for m in range(blocks):
            block = y1block(m)
            for c in range(r // rs.shape[1]):
                buf[m * (r // rs.shape[1]) + c] = block[c * rs.shape[1] : (c + 1) * rs.shape[1]]
        rs[comm.lon] = buf[comm.lon]
        first = comm.start("lon", lambda peer: buf.at[peer], lambda owner: rs.at[owner])

    def turn(low, high):
        for b in range(low, high):
            cell = z1[b]
            z1t[b] = stacked(jnp.concatenate([cell[:, :nj], cell[:, nj:]], axis=0).T, 1)

    turns = tuple(functools.partial(turn, r * k // 3, r * (k + 1) // 3) for k in range(3))
    finish_reduce(comm, first, rs, zs, ag, turns)

    acc = jnp.zeros((2 * r, ni), F32)
    for m in range(blocks):
        acc = acc + dot1(left_operand(ag[pl.ds(m * r, r), :]), yx[m], NT)
    acc = fold_rows(acc)
    b1s[comm.lat] = acc
    w = comm.gather("lat", b1s)
    comm.wait(w)
    b1t = total(b1s)

    bh, bl = split(jnp.concatenate([b1t] * per, axis=0).T)
    b1x = jnp.concatenate([
        jnp.concatenate([bh, bh], axis=0),
        jnp.concatenate([bl, jnp.zeros_like(bl)], axis=0),
    ], axis=1)

    def y2piece(p):
        cells = jnp.concatenate([z1t[p * per + g] for g in range(per)], axis=0)
        both = dot1(cells, b1x)
        both = both[:, :wide] + both[:, wide:]
        out = both[:nj]
        for g in range(1, per):
            out = jnp.where(lane(nj, wide) == g, both[g * nj : (g + 1) * nj], out)
        return out

    w = comm.scatter("lon", y2piece, y2s, y2r)
    g1s[comm.lon] = mmh(b1t, b1t, NT)
    g1w = comm.gather("lon", g1s)
    comm.wait(w)
    y2 = split(total(y2r))
    p2z[comm.lat] = dot3(split(vt), y2)
    w = comm.gather("lat", p2z)
    comm.wait(g1w)
    small[0] = chol_inverse(total(g1s))
    l1 = small[0]
    bd1 = split(block_diag(mmh(l1, l1, TN), per))
    lont = mmh(l1, b1t)
    lon_ref[...] = lont
    lonx = left_operand(lont)
    y2m = split(dot3(y2, bd1))

    def contract_lon(low, high):
        for j in range(low, high, 2):
            pair = jnp.concatenate(
                [stacked(t_ref[:, j, :], 0), stacked(t_ref[:, j + 1, :], 0)], axis=1
            )
            out = fold_rows(dot1(lonx, pair))
            xs[:, j, :] = out[:, :nr]
            xs[:, j + 1, :] = out[:, nr:]

    contract_lon(0, CUT)
    comm.wait(w)
    b2s[comm.lon] = dot3(split(total(p2z)), y2m, NT)
    w = comm.gather("lon", b2s)
    contract_lon(CUT, nj)
    for a in range(r):
        xh[a] = stacked(xs[a], 0)
    comm.wait(w)
    b2t = total(b2s)
    b2x = left_operand(b2t)
    parts = y3s.shape[0]
    half = per // parts

    def y3piece(h, p):
        outs = []
        first = p * per + h * half
        for g in range(0, half, 2):
            mates = [xh[first + k] for k in range(g, min(g + 2, half))]
            out = fold_rows(dot1(b2x, jnp.concatenate(mates, axis=1)))
            outs += [out[:, nr * k : nr * (k + 1)] for k in range(len(mates))]
        return jnp.concatenate(outs, axis=0)

    ws = [
        comm.scatter("lon", functools.partial(y3piece, h), y3s.at[h], y3r.at[h])
        for h in range(parts)
    ]
    g2s[comm.lat] = mmh(b2t, b2t, NT)
    g2w = comm.gather("lat", g2s)
    for h in range(parts):
        comm.wait(ws[h])
        y3z[h, comm.lat] = total(y3r.at[h])
        ws[h] = comm.gather("lat", y3z.at[h])
    comm.wait(g2w)
    small[1] = chol_inverse(total(g2s))
    l2 = small[1]
    bd2 = split(block_diag(l2, per))
    md2 = split(block_diag(mmh(l2, l2, TN), per))
    latt = mmh(l2, b2t)
    lat_ref[...] = latt
    for w in ws:
        comm.wait(w)
    whole = jnp.concatenate([total(y3z.at[h]) for h in range(parts)], axis=0)
    whole = split(whole)
    p3 = dot3(wts, whole, NT)
    y3m = dot3(md2, whole)
    b3s[comm.lon] = mm(p3, y3m)
    w = comm.gather("lon", b3s)
    y3 = split(dot3(bd2, whole))
    comm.wait(w)
    b3t = total(b3s)
    us[comm.lon] = dot3(split(b3t), y3, NT)
    w = comm.gather("lon", us)
    small[0] = chol_inverse(mmh(b3t, b3t, NT))
    l3 = small[0]
    radt = mm(l3, b3t)
    rad_ref[...] = radt
    back_high, back_low = split(mm(l3, radt, TN))
    back = jnp.concatenate([back_high, back_high, back_low], axis=0)
    l3h = split(l3)
    lonb = left_operand(lont.T)
    comm.wait(w)
    for p in range(nl):
        high, low = split(us[p])
        cells = jnp.concatenate([high, low, high], axis=0)
        f_ref[pl.ds(p * per, per)] = dot1(cells, back, TN).reshape(per, r, nr)
    for b in range(0, r, 2):
        pair = jnp.concatenate([stacked(f_ref[:, b + e, :], 0) for e in range(2)], axis=1)
        out = fold_rows(dot1(lonb, pair))
        x3[:, b, :] = out[:, :nr]
        x3[:, b + 1, :] = out[:, nr:]
    for p in range(nl):
        core_ref[pl.ds(p * wide, wide), :] = dot3(l3h, split(us[p])).T
    out_copy.wait()
    comm.finish()


def error_kernel(t_ref, s_ref, lon_ref, lat_ref, rad_ref, core_ref,
                 temp_out, err_out, lon_out, lat_out, rad_out, core_out, err, sem, temp_sem):
    temp_copy = pltpu.make_async_copy(t_ref, temp_out, temp_sem)
    temp_copy.start()
    latx = left_operand(lat_ref[...].T)
    ni, _, nr = t_ref.shape
    at = 32

    def chunk(c):
        part = pl.ds(c * at, at)
        return pltpu.make_async_copy(err.at[part], err_out.at[part], sem.at[c])

    @pl.loop(0, ni // at)
    def _(c):
        outs = []
        for k in range(0, at, 2):
            mates = [stacked(s_ref[c * at + k + e], 0) for e in range(2)]
            both = fold_rows(dot1(latx, jnp.concatenate(mates, axis=1)))
            outs += [both[:, :nr], both[:, nr:]]
        for k, out in enumerate(outs):
            err[c * at + k] = t_ref[c * at + k] - out
        chunk(c).start()

    lon_out[...] = lon_ref[...]
    lat_out[...] = lat_ref[...]
    rad_out[...] = rad_ref[...]
    core_out[...] = core_ref[...]

    @pl.loop(0, ni // at)
    def _(c):
        chunk(c).wait()

    temp_copy.wait()


def local(t, k, q, u, v, w):
    nl, nz = lax.axis_size("lon"), lax.axis_size("lat")
    ni, nj, nr = t.shape
    r = u.shape[1]
    rows = r * r * r // 128
    piece = rows // nl
    blocks = r * r // 128
    most = max(nl, nz)
    vm = pl.BlockSpec(memory_space=pltpu.VMEM)
    sds = lambda *s: jax.ShapeDtypeStruct(s, F32)
    V = lambda *s: pltpu.VMEM(s, F32)
    phases = 11 + 2 * PARTS
    per = r // nl
    wide = per * r
    B = lambda *s: pltpu.VMEM(s, BF16)
    parts = min(PARTS, per)
    cut = lambda n: (parts, n, wide // parts, nr)
    small = (sds(r, ni), sds(r, nj), sds(r, nr), sds(r * r, r))
    temp, s, lon, lat, rad, core = pl.pallas_call(
        functools.partial(sweep_kernel, nl, nz),
        out_shape=(sds(ni, nj, nr), sds(ni, r, nr)) + small,
        in_specs=[pl.BlockSpec(memory_space=pltpu.HBM)] * 6,
        out_specs=(pl.BlockSpec(memory_space=pl.ANY),) + (vm,) * 5,
        scratch_shapes=[
            V(ni, nj, nr), V(ni, nj, nr), V(r, ni), V(r, nj), V(r, nr),
            V(ni, nj, nr), V(ni, nj, nr), V(ni + 1, nj, nr), V(ni, nj, nr), V(ni, nj, nr),
            V(2, ni, nr), V(STEPS + 1, 2, nj, nr), V(STEPS + 1, 2, ni, nr), V(STEPS + 2, 2, ni, nr),
            V(2, 5, ni, nr), V(r, ni // 2, 2 * nj), B(r, nj, 2 * ni), V(r, nj, nr), B(r, 2 * nj, nr), V(r, r, nr),
            B(blocks, ni, 256), V(2, r, r),
            V(nl, nj, wide), V(nl, nj, wide), V(nz, r, wide),
            V(*cut(nl)), V(*cut(nl)), V(*cut(nz)), V(nl, r, wide),
            V(nz, r, ni), V(nl, r, nj), V(nl, r, nr),
            V(nl, r, r), V(nz, r, r),
            V(nl, piece, 128), V(nl, piece, 128), V(nz, piece, 128), V(rows, 128),
            pltpu.SemaphoreType.DMA((phases, most)),
            pltpu.SemaphoreType.DMA((phases, most)),
            pltpu.SemaphoreType.DMA((STEPS + 1, 4)),
            pltpu.SemaphoreType.DMA((STEPS + 1, 4)),
            pltpu.SemaphoreType.DMA,
            pltpu.SemaphoreType.DMA((6, 4)),
        ],
        compiler_params=pltpu.CompilerParams(
            collective_id=1, has_side_effects=True, vmem_limit_bytes=48 * 1024 * 1024
        ),
    )(*(pltpu.with_memory_space_constraint(x, pltpu.HBM) for x in (t, k, q, u.T, v.T, w.T)))
    anywhere = pl.BlockSpec(memory_space=pl.ANY)
    temp, err, lon, lat, rad, core = pl.pallas_call(
        error_kernel,
        out_shape=(sds(ni, nj, nr), sds(ni, nj, nr)) + small,
        in_specs=[vm] * 6,
        out_specs=(anywhere, anywhere) + (vm,) * 4,
        scratch_shapes=[
            V(ni, nj, nr), pltpu.SemaphoreType.DMA((ni // 32,)), pltpu.SemaphoreType.DMA
        ],
        compiler_params=pltpu.CompilerParams(vmem_limit_bytes=12 * 1024 * 1024),
    )(temp, s, lon, lat, rad, core)
    return temp, err, lon.T, lat.T, rad.T, core.reshape(r, r, r)


def solution(mesh):
    grid = P("lon", "lat", None)
    in_specs = (grid, grid, grid, P("lon", None), P("lat", None), P())
    out_specs = (grid, grid, P("lon", None), P("lat", None), P(), P())
    return jax.shard_map(local, mesh=mesh, in_specs=in_specs, out_specs=out_specs, check_vma=False)
```
